256 devices in a mesh: pair: 32 (over x, z_hi, core), pw: 8 (over y, z_lo).
Axes of the slice: x: 4, y: 4, z: 8 (z_hi: 4, z_lo: 2; z = z_hi * 2 + z_lo), core: 2. Of those that a mesh axis runs over, the one named last changes fastest.
Arguments:
- screened: bfloat16 [32, 4096, 4096], P('pair', 'pw'), may hold values from -0.09375 to 0.09375
- density: bfloat16 [32, 4096, 256], P('pair', 'pw'), may hold values from -0.75 to 0.75
- transform: bfloat16 [128, 256, 256], P('pw'), may hold values from -0.375 to 0.375
- energy: float32 [32768], P('pw'), may hold values from -1 to 1
- trial: bfloat16 [32768, 128], P('pw'), may hold values from -6 to 6
- coarse_index: int32 [128, 128, 4], P('pair', 'pw'), may hold values from 0 to 31, as said below
- interp_weight: bfloat16 [128, 128, 4], P('pair', 'pw'), may hold values from 0.1 to 1, as said below
- bands: int32 [128], replicated, may hold values from 8 to 16, as said below
Outputs:
- first_step: bfloat16 [32768, 128], P('pair')
- second_step: float32 [32768, 128], P('pw')
The draws below stay inside these ranges and needn't reach their ends.
Inputs may be any that keep to these rules, and one draw needn't show every extreme that they name: coarse_index[k, q, j] equals coarse_index[q, k, j]. interp_weight[k, q, j] equals interp_weight[q, k, j]. Some fine k-point has all 16 conduction bands live.
All inputs are finite; a program needn't handle non-finite values.
Results may differ from the reference program's by a relative error of at most 0.01.
Values may be sent and summed in bfloat16 or wider, within the bound.
A program may use at most 128 MiB of HBM per device.

```python
import math
import jax
import jax.numpy as jnp
from jax import lax

PWAVES = 4096
NCOND = 16
TRANS = 256
NTRIAL = 128
NNB = 4
COARSE = 32
NFINE = 128
NH = 32768


def mirror_pairs(table):
    upper_half = (jnp.arange(NFINE)[:, None] <= jnp.arange(NFINE)[None, :])[:, :, None]
    return jnp.where(upper_half, table, jnp.transpose(table, (1, 0, 2)))


def draw_coarse_index(key, part):
    draw_one = jax.random.randint(jax.random.fold_in(key, 11), (NFINE, NFINE, NNB), 0, COARSE)
    draw_two = jax.random.randint(jax.random.fold_in(key, 12), (NFINE, NFINE, NNB), 0, COARSE)
    pair_table = mirror_pairs(jnp.minimum(draw_one, draw_two))
    pair_table = pair_table.at[0, 0, 0].set(COARSE - 1)
    pair_table = pair_table.at[0, 0, 1].set(0)
    return pair_table.astype(jnp.int32)


def draw_interp_weight(key, part):
    uniform_part = jax.random.uniform(jax.random.fold_in(key, 21), (NFINE, NFINE, NNB), jnp.float32, 0.0, 1.0)
    values = 0.25 + 0.75 * uniform_part
    return mirror_pairs(values).astype(jnp.bfloat16)


def draw_bands(key, part):
    counts = jax.random.randint(jax.random.fold_in(key, 31), (NFINE,), NCOND // 2, NCOND + 1)
    full_spot = jax.random.randint(jax.random.fold_in(key, 32), (), 0, NFINE)
    return counts.at[full_spot].set(NCOND).astype(jnp.int32)


def level_of(key, extent, pieces, smallest, largest):
    def one(axis_at, blocks):
        draws = jax.random.uniform(jax.random.fold_in(jax.random.fold_in(key, 6), axis_at), (blocks,), jnp.float32, smallest / len(pieces), largest / len(pieces))
        return jnp.repeat(jnp.exp(draws), extent[axis_at] // blocks).reshape((-1,) + (1,) * (len(extent) - axis_at - 1))

    gain = one(*pieces[0])
    for cut in pieces[1:]:
        gain = gain * one(*cut)
    return gain


def noise(own_key, dims, spread, limit, cuts=(), kind=jnp.bfloat16):
    values = jax.random.normal(own_key, dims, jnp.float32) * spread
    if len(cuts) > 0:
        values = level_of(own_key, dims, cuts, -0.22, 0.18) * values
    return jnp.clip(values, min=-limit, max=limit).astype(kind)


def setup_inputs(seed: int = 0) -> dict:
    streams_of = jax.random.split(jax.random.key(seed), 9)
    screened = noise(streams_of[0], (COARSE, PWAVES, PWAVES), PWAVES ** -0.5, 0.09375, ((0, 32), (1, 8)))
    density = noise(streams_of[1], (COARSE, PWAVES, TRANS), 0.125, 0.75, ((0, 32), (1, 8)))
    transform = noise(streams_of[2], (NFINE, TRANS, TRANS), TRANS ** -0.5, 0.375, ((0, 8),))
    energy = jnp.clip(jax.random.uniform(streams_of[3], (NH,), jnp.float32, -1.0, 1.0) * level_of(streams_of[3], (NH,), ((0, 8),), -0.4, 0.0), -1.0, 1.0)
    trial = noise(streams_of[4], (NH, NTRIAL), 1.0, 6.0, ((0, 8),))
    coarse_index = draw_coarse_index(jax.random.fold_in(streams_of[8], 71), 0)
    interp_weight = draw_interp_weight(jax.random.fold_in(streams_of[8], 71), 0)
    bands = draw_bands(jax.random.fold_in(streams_of[8], 71), 0)
    return {"screened": screened, "density": density, "transform": transform, "energy": energy, "trial": trial, "coarse_index": coarse_index, "interp_weight": interp_weight, "bands": bands}


def coarse_block(operands):
    screened_one, density_one = operands
    applied = jnp.dot(screened_one, density_one, preferred_element_type=jnp.float32).astype(jnp.bfloat16)
    raw_sum = jnp.dot(density_one.T, applied, preferred_element_type=jnp.float32)
    return (0.5 * (raw_sum + raw_sum.T)).astype(jnp.bfloat16)

def reference(screened, density, transform, energy, trial, coarse_index, interp_weight, bands):
    kernel = lax.map(coarse_block, (screened, density))
    live_mask = ((jnp.arange(TRANS) % NCOND)[None, :] < bands[:, None]).astype(jnp.float32)
    norm_scale = 1.0 / math.sqrt(NFINE * TRANS)
    energies = energy.reshape(NFINE, TRANS)
    identity = jnp.eye(TRANS, dtype=jnp.float32)
    transform_wide = transform.astype(jnp.float32)

    def row_block(point):
        neighbours = coarse_index[point]
        picked = kernel[neighbours].astype(jnp.float32)
        mixture = jnp.einsum('bj,bjst->bst', interp_weight[point].astype(jnp.float32), picked).astype(jnp.bfloat16)
        turned = jnp.einsum('bst,btu->bsu', mixture.astype(jnp.float32), transform_wide).astype(jnp.bfloat16)
        blocks = jnp.einsum('sv,bsu->vbu', transform_wide[point], turned.astype(jnp.float32))
        blocks = blocks * live_mask[point][:, None, None] * live_mask[None, :, :] * norm_scale
        same_point = (jnp.arange(NFINE) == point).astype(jnp.float32)
        diagonal_part = identity[:, None, :] * (energies * same_point[:, None])[None, :, :]
        return (blocks + diagonal_part).astype(jnp.bfloat16).reshape(TRANS, NFINE * TRANS)
    hamiltonian = lax.map(row_block, jnp.arange(NFINE)).reshape(NFINE * TRANS, NFINE * TRANS)
    first_step = jnp.dot(hamiltonian, trial, preferred_element_type=jnp.float32).astype(jnp.bfloat16)
    second_step = 2.0 * jnp.dot(hamiltonian.T, first_step, preferred_element_type=jnp.float32) - trial.astype(jnp.float32)
    return (first_step, second_step)
```

```python
import math

import jax
import jax.numpy as jnp
from jax import lax
from jax.experimental import pallas as pl
from jax.experimental.pallas import tpu as pltpu
from jax.sharding import PartitionSpec as P

MESH = pl.DeviceIdType.MESH
BF = jnp.bfloat16
F32 = jnp.float32
NCOND = 16


def dot(lhs, rhs):
    return jnp.dot(lhs, rhs, preferred_element_type=F32)


def dot_t(lhs, rhs):
    return lax.dot_general(lhs, rhs, (((1,), (1,)), ((), ())), preferred_element_type=F32)


def iota(shape, dim):
    return lax.broadcasted_iota(jnp.int32, shape, dim)


def kernel(
    w_hbm, d_hbm, t_hbm, x_hbm, live_ref, energy_ref, tab_ref,
    out1, out2,
    wv, dv, tv, xv, acc, kp, kr, kt, kcat, tp, tq, ct, ucat, ysend, yrecv, zs, zr,
    rows_x, fs, fb, fbf, g, gf,
    sem_local, sa_s, sa_r, sb_s, sb_r, sy_s, sy_r, sk_s, sk_r, sz_s, sz_r, sq_s, sq_r,
    sg_s, sg_r, sf_s, sf_r,
):
    a = lax.axis_index("pair")
    b = lax.axis_index("pw")
    x, zh, core = a // 8, (a // 2) % 4, a % 2
    y, zl = b // 2, b % 2
    b_p = ((y + 1) % 4) * 2 + zl
    b_m = ((y + 3) % 4) * 2 + zl
    b_f = ((y + 2) % 4) * 2 + zl
    b_z = y * 2 + 1 - zl
    b_pz = ((y + 1) % 4) * 2 + 1 - zl
    b_mz = ((y + 3) % 4) * 2 + 1 - zl
    b_fz = ((y + 2) % 4) * 2 + 1 - zl
    pending = []

    def pair_z(j):
        return x * 8 + ((zh + j) % 4) * 2 + core

    def pair_x(j):
        return ((x + j) % 4) * 8 + zh * 2 + core

    pair_c = x * 8 + zh * 2 + 1 - core

    def send(src, dst, s_sem, r_sem, pair=None, pw=None):
        copy = pltpu.make_async_remote_copy(
            src_ref=src, dst_ref=dst, send_sem=s_sem, recv_sem=r_sem,
            device_id={"pair": a if pair is None else pair, "pw": b if pw is None else pw},
            device_id_type=MESH,
        )
        copy.start()
        return copy

    def arrived(slot, sem):
        pltpu.make_async_copy(slot, slot, sem).wait()

    barrier = pltpu.get_barrier_semaphore()
    for j in range(1, 8):
        pl.semaphore_signal(barrier, inc=1, device_id={"pair": a, "pw": (b + j) % 8}, device_id_type=MESH)
    for j in range(1, 4):
        pl.semaphore_signal(barrier, inc=1, device_id={"pair": pair_z(j), "pw": b}, device_id_type=MESH)
        pl.semaphore_signal(barrier, inc=1, device_id={"pair": pair_x(j), "pw": b}, device_id_type=MESH)
    pl.semaphore_signal(barrier, inc=1, device_id={"pair": pair_c, "pw": b}, device_id_type=MESH)
    x_load = pltpu.make_async_copy(x_hbm, xv, sem_local.at[0])
    t_load = pltpu.make_async_copy(t_hbm, tv, sem_local.at[1])
    d_loads = [
        pltpu.make_async_copy(d_hbm.at[0, pl.ds(h * 256, 256)], dv.at[2 * b + h], sem_local.at[2 + h]) for h in range(2)
    ]
    w_loads = [
        pltpu.make_async_copy(w_hbm.at[0, pl.ds(i * 128, 128)], wv.at[pl.ds(i * 128, 128)], sem_local.at[4 + i])
        for i in range(4)
    ]
    for load in [x_load, t_load, *d_loads, *w_loads]:
        load.start()
    tp[x, zh, core] = tab_ref[...]
    pl.semaphore_wait(barrier, 14)

    M0, M1, F0, MZ0, MZ1, P1, P0, F1, PZ0, PZ1, Z0, Z1, FZ0, FZ1 = range(14)
    sent = [0]

    def relay(src, slot, role, pw):
        pending.append(send(src, dv.at[slot], sa_s.at[sent[0]], sa_r.at[role], pw=pw))
        sent[0] += 1

    own = [d_hbm.at[0, pl.ds(h * 256, 256)] for h in range(2)]
    relay(own[0], 2 * b, M0, b_p)
    relay(own[1], 2 * b + 1, P1, b_m)
    relay(own[0], 2 * b, Z0, b_z)
    relay(own[1], 2 * b + 1, M1, b_p)
    relay(own[0], 2 * b, P0, b_m)
    relay(own[1], 2 * b + 1, Z1, b_z)

    def gather_z(buf, n):
        for j in range(1, 4):
            part = buf.at[x, zh, core]
            pending.append(send(part, part, sg_s.at[n, j - 1], sg_r.at[n, j - 1], pair=pair_z(j)))

    def gather_x(buf, n):
        for j in range(1, 4):
            arrived(buf.at[x, (zh + 4 - j) % 4, core], sg_r.at[n, j - 1])
        for j in range(1, 4):
            part = buf.at[x, :, core]
            pending.append(send(part, part, sg_s.at[n, 2 + j], sg_r.at[n, 2 + j], pair=pair_x(j)))

    def gather_core(buf, n):
        for j in range(1, 4):
            arrived(buf.at[(x + 4 - j) % 4, :, core], sg_r.at[n, 2 + j])
        part = buf.at[:, :, core]
        pending.append(send(part, part, sg_s.at[n, 6], sg_r.at[n, 6], pair=pair_c))

    def gather_end(buf, n):
        arrived(buf.at[:, :, 1 - core], sg_r.at[n, 6])

    gather_z(tp, 0)

    row_k = iota((64, 256), 0) % 16
    live = jnp.concatenate([live_ref[...]] * 4, axis=0)
    lane = iota((16, 128), 1)

    def transforms(rows, transposed):
        def step(k, total):
            mine = jnp.where(row_k == k, rows, 0.0).astype(BF)
            return total + (dot_t if transposed else dot)(mine, tv[k])

        return lax.fori_loop(0, 16, step, jnp.zeros((64, 256), F32), unroll=4)

    def spread_columns(app, rows):
        for part in range(8):
            i, half = part % 4, part // 4
            block = jnp.zeros((16, 128), F32)
            for n in range(4):
                piece = rows[n * 16 : n * 16 + 16, half * 128 : half * 128 + 128]
                shift = ((n - i) * 32) % 128
                if shift:
                    piece = pltpu.roll(piece, shift, axis=1)
                block = jnp.where(lane // 32 == n, piece, block)
            ysend[app, part] = block.astype(BF)
        yrecv[app, b] = ysend[app, b]
        for j in range(1, 8):
            dest = (b + j) % 8
            pending.append(
                send(ysend.at[app, dest], yrecv.at[app, b], sy_s.at[app, j - 1], sy_r.at[app, j - 1], pw=dest)
            )

    x_load.wait()
    chosen = (iota((8, 128), 1) == 4 * a + iota((8, 128), 0)) & (iota((8, 128), 0) < 4)
    chosen = chosen.astype(F32).astype(BF)
    for k in range(16):
        picked = dot_t(chosen, xv[k * 256 : (k + 1) * 256, :])
        for n in range(4):
            rows_x[n * 16 + k : n * 16 + k + 1, :] = picked[n : n + 1, :]
    t_load.wait()
    spread_columns(0, transforms(live * rows_x[...], True))

    def accumulate(slot, first=False):
        columns = pl.ds(pl.multiple_of(slot * 256, 256), 256)
        product = dot(wv[:, columns], dv[slot])
        if first:
            acc[...] = product
        else:
            acc[...] += product

    for load in [*d_loads, *w_loads]:
        load.wait()
    accumulate(2 * b, True)
    accumulate(2 * b + 1)
    arrived(dv.at[2 * b_m], sa_r.at[M0])
    relay(dv.at[2 * b_m], 2 * b_m, F0, b_p)
    arrived(dv.at[2 * b_p + 1], sa_r.at[P1])
    relay(dv.at[2 * b_p + 1], 2 * b_p + 1, F1, b_m)
    for h, role in ((0, Z0), (1, Z1)):
        slot = 2 * b_z + h
        arrived(dv.at[slot], sa_r.at[role])
        relay(dv.at[slot], slot, (MZ0, MZ1)[h], b_p)
        relay(dv.at[slot], slot, (PZ0, PZ1)[h], b_m)
    gather_x(tp, 0)
    for slot in (2 * b_m, 2 * b_p + 1, 2 * b_z, 2 * b_z + 1):
        accumulate(slot)
    for slot, role in ((2 * b_m + 1, M1), (2 * b_p, P0)):
        arrived(dv.at[slot], sa_r.at[role])
        accumulate(slot)
    gather_core(tp, 0)
    for h, role in ((0, F0), (1, F1)):
        slot = 2 * b_f + h
        arrived(dv.at[slot], sa_r.at[role])
        relay(dv.at[slot], slot, (FZ0, FZ1)[h], b_z)
    accumulate(2 * b_f)
    accumulate(2 * b_f + 1)

    gather_end(tp, 0)
    q_of = iota((128, 256), 0)
    pick = (iota((128, 256), 1) == (q_of // 4) * 8 + q_of % 4).astype(F32).astype(BF)
    tq[b] = dot(pick, tp[...].reshape(256, 128).astype(BF)).astype(BF)
    for j in range(1, 8):
        pending.append(send(tq.at[b], tq.at[b], sq_s.at[j - 1], sq_r.at[j - 1], pw=(b + j) % 8))

    for slot, role in (
        (2 * b_mz, MZ0), (2 * b_pz, PZ0), (2 * b_mz + 1, MZ1), (2 * b_pz + 1, PZ1), (2 * b_fz, FZ0), (2 * b_fz + 1, FZ1)
    ):
        arrived(dv.at[slot], sa_r.at[role])
        accumulate(slot)

    applied = acc[...].astype(BF)
    raw = jnp.zeros((256, 256), F32)
    for h in range(2):
        raw += lax.dot_general(
            dv[2 * b + h], applied[h * 256 : h * 256 + 256], (((0,), (0,)), ((), ())), preferred_element_type=F32
        )
    kp[...] = (0.5 * (raw + raw.T)).astype(BF).reshape(8, 32, 256)
    for j in range(1, 8):
        dest = (b + j) % 8
        pending.append(send(kp.at[dest], kr.at[b], sk_s.at[j - 1], sk_r.at[j - 1], pw=dest))
    kr[b] = kp[b]

    for j in range(1, 8):
        arrived(tq.at[(b + 8 - j) % 8], sq_r.at[j - 1])
    lanes = iota((128, 128), 1)
    index_parts, weight_parts = [], []
    for p in range(4):
        even = tq[2 * p].astype(F32)
        odd = tq[2 * p + 1].astype(F32)
        index_parts.append(jnp.where(lanes < 64, even, pltpu.roll(odd, 64, axis=1)))
        weight_parts.append(jnp.where(lanes < 64, pltpu.roll(even, 64, axis=1), odd))
    indexes = jnp.concatenate(index_parts, axis=1)
    weights = jnp.concatenate(weight_parts, axis=1)
    from_lane = iota((512, 128), 0)
    to_k = ((from_lane // 64) * 16 + from_lane % 16 == iota((512, 128), 1)).astype(F32).astype(BF)

    def coefficients(i, carry):
        for h in range(2):
            chosen_w = jnp.where(indexes == (2 * i + h).astype(F32), weights, 0.0).astype(BF)
            ct[i, :, h * 128 : h * 128 + 128] = dot(chosen_w, to_k).astype(BF)
        return carry

    lax.fori_loop(0, 16, coefficients, 0)

    for j in range(1, 8):
        arrived(kr.at[(b + 8 - j) % 8], sk_r.at[j - 1])
    total = kr[0].astype(F32)
    for j in range(1, 8):
        total += kr[j].astype(F32)
    kt[x, zh, core] = total.astype(BF)
    gather_z(kt, 1)

    def mix(app):
        for j in range(1, 8):
            arrived(yrecv.at[app, (b + 8 - j) % 8], sy_r.at[app, j - 1])
        columns = yrecv[app].reshape(128, 128).astype(F32).T.astype(BF)

        def step(i, carry):
            mixed = dot(columns, ct[i]).astype(BF)
            for h in range(2):
                for n in range(4):
                    ucat[2 * i + h, :, n * 128 : n * 128 + 128] = mixed[
                        n * 32 : n * 32 + 32, h * 128 : h * 128 + 128
                    ]
            return carry

        lax.fori_loop(0, 16, step, 0, unroll=2)

    def contract(app):
        product = dot(kcat[...], ucat[...].reshape(1024, 512))
        zs[app] = product.T.astype(BF).reshape(4, 128, 256)
        part = pl.ds(pl.multiple_of(b * 16, 16), 16)
        zr[app, b] = zs[app, :, part, :]
        for j in range(1, 8):
            dest = (b + j) % 8
            part = pl.ds(pl.multiple_of(dest * 16, 16), 16)
            pending.append(
                send(zs.at[app, :, part, :], zr.at[app, b], sz_s.at[app, j - 1], sz_r.at[app, j - 1], pw=dest)
            )

    def summed(app):
        for j in range(1, 8):
            arrived(zr.at[app, (b + 8 - j) % 8], sz_r.at[app, j - 1])
        rows = zr[app, 0].astype(F32)
        for j in range(1, 8):
            rows += zr[app, j].astype(F32)
        return rows.reshape(64, 256)

    norm_scale = 1.0 / math.sqrt(32768.0)
    energy = jnp.concatenate([energy_ref[...]] * 4, axis=0)

    def finish(app, vector):
        return norm_scale * live * transforms(summed(app), False) + energy * vector

    mix(0)
    gather_x(kt, 1)
    gather_core(kt, 1)
    gather_end(kt, 1)
    for i in range(8):
        rows = kt[i // 2, 2 * (i % 2) : 2 * (i % 2) + 2].reshape(128, 256)
        kcat[:, i * 128 : i * 128 + 128] = rows.astype(F32).T.astype(BF)
    contract(0)
    first = finish(0, rows_x[...]).astype(BF)
    first_wide = first.astype(F32)
    spread_columns(1, transforms(live * first_wide, True))

    r_in, r_out = iota((64, 64), 1), iota((64, 64), 0)
    order = (r_in == ((r_out // 4) % 4) * 16 + (r_out // 16) * 4 + r_out % 4).astype(F32).astype(BF)
    fs[...] = dot(order, first).astype(BF).reshape(4, 16, 256)
    first_sends = []
    for i in range(4):
        target = 4 * b + i

        @pl.when(target == a)
        def _():
            fb[a] = fs[i]

        @pl.when(target != a)
        def _():
            send(fs.at[i], fb.at[a], sf_s.at[i], sf_r.at[a], pair=target)

    mix(1)
    contract(1)

    root = a // 4
    d_y = (y + 4 - root // 2) % 4
    d_z = (zl + root % 2) % 2
    is_root = (d_y == 0) & (d_z == 0)
    odd = d_y % 2 == 1

    @pl.when(b == root)
    def _():
        def take(s, carry):
            @pl.when(s != a)
            def _():
                arrived(fb.at[s], sf_r.at[s])

            return carry

        lax.fori_loop(0, 32, take, 0)
        wide = fb[...].reshape(512, 256).astype(F32)
        for u in range(2):
            fbf[u] = wide[:, u * 128 : u * 128 + 128]
        for k in range(4):
            for u in range(2):
                at = k * 256 + u * 128
                out1[at : at + 128, :] = fbf[u, pl.ds(k, 128, stride=4), :].T.astype(BF)

    def half(h):
        return out1.at[pl.ds(h * 512, 512)]

    def pass_on(h, pw, slot):
        return pltpu.make_async_remote_copy(
            src_ref=half(h), dst_ref=half(h), send_sem=sb_s.at[slot], recv_sem=sb_r.at[h],
            device_id={"pair": a, "pw": pw}, device_id_type=MESH,
        )

    to_p = [pass_on(h, b_p, h) for h in range(2)]
    to_m = [pass_on(h, b_m, 2 + h) for h in range(2)]
    to_z = [pass_on(h, b_z, 4 + h) for h in range(2)]

    def take_halves():
        for h in range(2):
            arrived(half(h), sb_r.at[h])

    @pl.when(is_root)
    def _():
        for h in range(2):
            to_z[h].start()
            to_p[h].start()
            to_m[h].start()

    second = 2.0 * finish(1, first_wide) - rows_x[...]
    g[x, zh, core] = second.astype(BF)
    gather_z(g, 2)

    @pl.when((d_y == 0) & (d_z == 1))
    def _():
        take_halves()
        for h in range(2):
            to_p[h].start()
            to_m[h].start()

    @pl.when(odd & (d_z == 0))
    def _():
        take_halves()

    @pl.when((d_y == 1) & (d_z == 0))
    def _():
        to_p[0].start()

    @pl.when((d_y == 3) & (d_z == 0))
    def _():
        to_m[1].start()

    gather_x(g, 2)
    gather_core(g, 2)

    @pl.when(odd & (d_z == 1))
    def _():
        take_halves()

    @pl.when((d_y == 1) & (d_z == 1))
    def _():
        to_p[0].start()

    @pl.when((d_y == 3) & (d_z == 1))
    def _():
        to_m[1].start()

    gather_end(g, 2)
    wide = g[...].reshape(2048, 256).astype(F32)
    for u in range(2):
        gf[u] = wide[:, u * 128 : u * 128 + 128]

    def place(k, carry):
        for u in range(2):
            at = pl.multiple_of(k * 256 + u * 128, 128)
            out2[pl.ds(at, 128), :] = gf[u, pl.ds(k, 128, stride=16), :].T
        return carry

    lax.fori_loop(0, 16, place, 0, unroll=2)

    @pl.when(d_y == 2)
    def _():
        take_halves()

    for copy in pending:
        copy.wait_send()
    for i in range(4):
        target = 4 * b + i

        @pl.when(target != a)
        def _():
            pltpu.make_async_copy(fs.at[i], fs.at[i], sf_s.at[i]).wait()

    @pl.when(is_root)
    def _():
        for h in range(2):
            to_z[h].wait_send()

    @pl.when(d_y == 0)
    def _():
        for h in range(2):
            to_p[h].wait_send()
            to_m[h].wait_send()

    @pl.when(d_y == 1)
    def _():
        to_p[0].wait_send()

    @pl.when(d_y == 3)
    def _():
        to_m[1].wait_send()


def shards(screened, density, transform, energy, trial, coarse_index, interp_weight, bands):
    b = lax.axis_index("pw")
    positions = jnp.arange(256, dtype=jnp.int32) % NCOND
    own_bands = lax.dynamic_slice_in_dim(bands, b * 16, 16, 0)
    live = (positions[None, :] < own_bands[:, None]).astype(F32)
    energies = energy.reshape(16, 256)
    index_rows = jnp.transpose(coarse_index, (0, 2, 1)).reshape(4, 64).astype(F32)
    weight_rows = jnp.transpose(interp_weight, (0, 2, 1)).reshape(4, 64).astype(F32)
    table = jnp.pad(jnp.concatenate([index_rows, weight_rows], axis=1), ((0, 4), (0, 0)))
    hbm = pl.BlockSpec(memory_space=pl.ANY)
    vmem = pl.BlockSpec(memory_space=pltpu.VMEM)
    dma = pltpu.SemaphoreType.DMA
    return pl.pallas_call(
        kernel,
        out_shape=(jax.ShapeDtypeStruct((1024, 128), BF), jax.ShapeDtypeStruct((4096, 128), F32)),
        in_specs=[hbm] * 4 + [vmem] * 3,
        out_specs=(vmem, vmem),
        scratch_shapes=[
            pltpu.VMEM((512, 4096), BF),
            pltpu.VMEM((16, 256, 256), BF),
            pltpu.VMEM((16, 256, 256), BF),
            pltpu.VMEM((4096, 128), BF),
            pltpu.VMEM((512, 256), F32),
            pltpu.VMEM((8, 32, 256), BF),
            pltpu.VMEM((8, 32, 256), BF),
            pltpu.VMEM((4, 4, 2, 32, 256), BF),
            pltpu.VMEM((256, 1024), BF),
            pltpu.VMEM((4, 4, 2, 8, 128), F32),
            pltpu.VMEM((8, 128, 128), BF),
            pltpu.VMEM((16, 128, 256), BF),
            pltpu.VMEM((32, 32, 512), BF),
            pltpu.VMEM((2, 8, 16, 128), BF),
            pltpu.VMEM((2, 8, 16, 128), BF),
            pltpu.VMEM((2, 4, 128, 256), BF),
            pltpu.VMEM((2, 8, 4, 16, 256), BF),
            pltpu.VMEM((64, 256), F32),
            pltpu.VMEM((4, 16, 256), BF),
            pltpu.VMEM((32, 16, 256), BF),
            pltpu.VMEM((2, 512, 128), F32),
            pltpu.VMEM((4, 4, 2, 64, 256), BF),
            pltpu.VMEM((2, 2048, 128), F32),
            dma((8,)),
            dma((14,)), dma((14,)),
            dma((6,)), dma((2,)),
            dma((2, 7)), dma((2, 7)),
            dma((7,)), dma((7,)),
            dma((2, 7)), dma((2, 7)),
            dma((7,)), dma((7,)),
            dma((3, 7)), dma((3, 7)),
            dma((4,)), dma((32,)),
        ],
        compiler_params=pltpu.CompilerParams(
            collective_id=0, has_side_effects=True, vmem_limit_bytes=60 * 1024 * 1024
        ),
        name="bse_chebyshev",
    )(screened, density, transform, trial, live, energies, table)


def solution(mesh):
    in_specs = (
        P("pair", "pw", None),
        P("pair", "pw", None),
        P("pw", None, None),
        P("pw"),
        P("pw", None),
        P("pair", "pw", None),
        P("pair", "pw", None),
        P(),
    )
    out_specs = (P("pair", None), P("pw", None))
    return jax.shard_map(shards, mesh=mesh, in_specs=in_specs, out_specs=out_specs, check_vma=False)
```

```python
import math

import jax
import jax.numpy as jnp
from jax import lax
from jax.experimental import pallas as pl
from jax.experimental.pallas import tpu as pltpu
from jax.sharding import PartitionSpec as P

MESH = pl.DeviceIdType.MESH
BF = jnp.bfloat16
F32 = jnp.float32
NCOND = 16


def dot(lhs, rhs):
    return jnp.dot(lhs, rhs, preferred_element_type=F32)


def dot_t(lhs, rhs):
    return lax.dot_general(lhs, rhs, (((1,), (1,)), ((), ())), preferred_element_type=F32)


def iota(shape, dim):
    return lax.broadcasted_iota(jnp.int32, shape, dim)


def kernel(
    w_hbm, d_hbm, t_hbm, x_hbm, bands_hbm, energy_hbm, index_hbm, weight_hbm,
    out1, g,
    wv, dv, tv, xv, acc, kp, kr, kt, kcat, tab, tb, t2, t2f, ct, ucat, ysend, yrecv, zs, zr,
    rows_x, fs, fb, fbf, bands_ref, energy_ref, index_ref, weight_ref,
    sem_local, sa_s, sa_r, sb_s, sb_r, sy_s, sy_r, sk_s, sk_r, sz_s, sz_r, sq_s, sq_r,
    sg_s, sg_r, sf_s, sf_r,
):
    a = lax.axis_index("pair")
    b = lax.axis_index("pw")
    x, zh, core = a // 8, (a // 2) % 4, a % 2
    y, zl = b // 2, b % 2
    b_p = ((y + 1) % 4) * 2 + zl
    b_m = ((y + 3) % 4) * 2 + zl
    b_f = ((y + 2) % 4) * 2 + zl
    b_z = y * 2 + 1 - zl
    b_pz = ((y + 1) % 4) * 2 + 1 - zl
    b_mz = ((y + 3) % 4) * 2 + 1 - zl
    b_fz = ((y + 2) % 4) * 2 + 1 - zl
    pw_out = (b_fz, b_f, b_pz, b_mz, b_p, b_m, b_z)
    pw_in = (b_fz, b_f, b_mz, b_pz, b_m, b_p, b_z)
    pending = []

    pair_c = x * 8 + zh * 2 + 1 - core

    def send(src, dst, s_sem, r_sem, pair=None, pw=None):
        copy = pltpu.make_async_remote_copy(
            src_ref=src, dst_ref=dst, send_sem=s_sem, recv_sem=r_sem,
            device_id={"pair": a if pair is None else pair, "pw": b if pw is None else pw},
            device_id_type=MESH,
        )
        copy.start()
        return copy

    def arrived(slot, sem):
        pltpu.make_async_copy(slot, slot, sem).wait()

    barrier = pltpu.get_barrier_semaphore()
    peers = [(x * 8 + ((zh + 2) % 4) * 2 + core, b)] + [(a, dest) for dest in pw_out]
    peers += [(((x + j) % 4) * 8 + zh * 2 + core, b) for j in (2, 1, 3)]
    peers += [(x * 8 + ((zh + j) % 4) * 2 + core, b) for j in (1, 3)] + [(pair_c, b)]
    for pair, pw in peers:
        pl.semaphore_signal(barrier, inc=1, device_id={"pair": pair, "pw": pw}, device_id_type=MESH)
    x_load = pltpu.make_async_copy(x_hbm, xv, sem_local.at[0])
    t_load = pltpu.make_async_copy(t_hbm, tv, sem_local.at[1])
    d_loads = [
        pltpu.make_async_copy(d_hbm.at[0, pl.ds(h * 256, 256)], dv.at[2 * b + h], sem_local.at[2 + h]) for h in range(2)
    ]
    w_loads = [
        pltpu.make_async_copy(w_hbm.at[0, pl.ds(i * 128, 128)], wv.at[pl.ds(i * 128, 128)], sem_local.at[4 + i])
        for i in range(4)
    ]
    x_load.start()
    small_loads = [
        pltpu.make_async_copy(src, dst, sem_local.at[8 + i])
        for i, (src, dst) in enumerate((
            (index_hbm, index_ref), (weight_hbm, weight_ref), (bands_hbm, bands_ref), (energy_hbm, energy_ref)
        ))
    ]
    for load in small_loads:
        load.start()
    for load in small_loads:
        load.wait()

    tab[...] = jnp.zeros_like(tab)
    tab[:, 0:4, 0:16] = index_ref[...].astype(F32)
    tab[:, 4:8, 0:16] = weight_ref[...].astype(F32)
    tb[b] = tab[...].reshape(32, 128).astype(BF)
    own_bands = jnp.where(iota((16, 128), 1) == 16 * b + iota((16, 128), 0), bands_ref[...].astype(F32), 0.0)
    own_bands = jnp.sum(own_bands, axis=1, keepdims=True)
    live = ((iota((16, 256), 1) % NCOND).astype(F32) < own_bands).astype(F32)
    live = jnp.concatenate([live] * 4, axis=0)
    energy = jnp.concatenate([energy_ref[pl.ds(u, 16, stride=2), :] for u in range(2)], axis=1)
    energy = jnp.concatenate([energy] * 4, axis=0)
    chosen = (iota((8, 128), 1) == 4 * a + iota((8, 128), 0)) & (iota((8, 128), 0) < 4)
    chosen = chosen.astype(F32).astype(BF)
    x_load.wait()
    for load in [t_load, *d_loads, *w_loads]:
        load.start()
    for k in range(16):
        picked = dot_t(chosen, xv[k * 256 : (k + 1) * 256, :])
        for n in range(4):
            rows_x[n * 16 + k : n * 16 + k + 1, :] = picked[n : n + 1, :]
    pl.semaphore_wait(barrier, len(peers))

    for j, dest in enumerate(pw_out):
        pending.append(send(tb.at[b], tb.at[b], sq_s.at[j], sq_r.at[j], pw=dest))

    M0, M1A, M1B, F0, MZ0, MZ1, P1, P0A, P0B, F1, PZ0, PZ1, Z0, Z1, FZ0, FZ1 = range(16)
    sent = [0]

    def relay(src, dst, role, pw):
        pending.append(send(src, dst, sa_s.at[sent[0]], sa_r.at[role], pw=pw))
        sent[0] += 1

    def quarter(h, r):
        return dv.at[2 * b + h, pl.ds(r * 128, 128)]

    own = [d_hbm.at[0, pl.ds(h * 256, 256)] for h in range(2)]
    quarters = [[d_hbm.at[0, pl.ds(h * 256 + r * 128, 128)] for r in range(2)] for h in range(2)]
    relay(own[0], dv.at[2 * b], M0, b_p)
    relay(own[1], dv.at[2 * b + 1], P1, b_m)
    relay(own[0], dv.at[2 * b], Z0, b_z)
    relay(quarters[1][0], quarter(1, 0), M1A, b_p)
    relay(quarters[0][0], quarter(0, 0), P0A, b_m)
    relay(own[1], dv.at[2 * b + 1], Z1, b_z)

    z_of = (zh, (zh + 1) % 4, (zh + 3) % 4, (zh + 2) % 4)
    x_of = (x, (x + 1) % 4, (x + 3) % 4, (x + 2) % 4)
    from_of = (0, 2, 1, 3)

    def gather(buf, n):
        def move(part, index, pair):
            pending.append(send(part, part, sg_s.at[n, index], sg_r.at[n, index], pair=pair))

        def x_out(p):
            for i in (3, 1, 2):
                move(buf.at[x, z_of[p], core], 3 * p + i + 2, x_of[i] * 8 + zh * 2 + core)

        def x_in(p):
            for i in (1, 2, 3):
                arrived(buf.at[x_of[i], z_of[p], core], sg_r.at[n, 3 * p + from_of[i] + 2])
            move(buf.at[:, z_of[p], core], 15 + p, pair_c)

        def z_in(i):
            arrived(buf.at[x, z_of[i], core], sg_r.at[n, from_of[i] - 1])
            x_out(i)

        for i in (3, 1, 2):
            move(buf.at[x, zh, core], i - 1, x * 8 + z_of[i] * 2 + core)
        x_out(0)
        yield
        z_in(1)
        z_in(2)
        yield
        z_in(3)
        x_in(0)
        yield
        x_in(1)
        x_in(2)
        x_in(3)
        yield
        for p in range(4):
            arrived(buf.at[:, z_of[p], 1 - core], sg_r.at[n, 15 + p])
        yield

    row_k = iota((64, 256), 0) % 16
    lane = iota((16, 128), 1)

    def transforms(rows, transposed):
        def step(k, total):
            mine = jnp.where(row_k == k, rows, 0.0).astype(BF)
            return total + (dot_t if transposed else dot)(mine, tv[k])

        return lax.fori_loop(0, 16, step, jnp.zeros((64, 256), F32), unroll=4)

    def spread_columns(app, rows):
        for part in range(8):
            i, half = part % 4, part // 4
            block = jnp.zeros((16, 128), F32)
            for n in range(4):
                piece = rows[n * 16 : n * 16 + 16, half * 128 : half * 128 + 128]
                shift = ((n - i) * 32) % 128
                if shift:
                    piece = pltpu.roll(piece, shift, axis=1)
                block = jnp.where(lane // 32 == n, piece, block)
            ysend[app, part] = block.astype(BF)
        yrecv[app, b] = ysend[app, b]
        for j, dest in enumerate(pw_out):
            pending.append(send(ysend.at[app, dest], yrecv.at[app, b], sy_s.at[app, j], sy_r.at[app, j], pw=dest))

    t_load.wait()
    spread_columns(0, transforms(live * rows_x[...], True))

    def accumulate(slot, first=False):
        columns = pl.ds(pl.multiple_of(slot * 256, 256), 256)
        product = dot(wv[:, columns], dv[slot])
        if first:
            acc[...] = product
        else:
            acc[...] += product

    arrived(dv.at[2 * b_m], sa_r.at[M0])
    relay(dv.at[2 * b_m], dv.at[2 * b_m], F0, b_p)
    relay(quarters[1][1], quarter(1, 1), M1B, b_p)
    arrived(dv.at[2 * b_p + 1], sa_r.at[P1])
    relay(dv.at[2 * b_p + 1], dv.at[2 * b_p + 1], F1, b_m)
    relay(quarters[0][1], quarter(0, 1), P0B, b_m)

    table_lane = iota((32, 128), 1) // 16
    table_rows = jnp.zeros((32, 128), F32)
    for j, source in enumerate(pw_in):
        arrived(tb.at[source], sq_r.at[j])
    for s in range(8):
        piece = tb[s].astype(F32)
        if s:
            piece = pltpu.roll(piece, 16 * s, axis=1)
        table_rows = jnp.where(table_lane == s, piece, table_rows)
    t2[x, zh, core] = table_rows.astype(BF)
    table_gather = gather(t2, 0)
    next(table_gather)

    for h, role in ((0, Z0), (1, Z1)):
        slot = 2 * b_z + h
        arrived(dv.at[slot], sa_r.at[role])
        relay(dv.at[slot], dv.at[slot], (MZ0, MZ1)[h], b_p)
        relay(dv.at[slot], dv.at[slot], (PZ0, PZ1)[h], b_m)
    for load in [*d_loads, *w_loads]:
        load.wait()
    accumulate(2 * b, True)
    accumulate(2 * b + 1)
    for h, role in ((0, F0), (1, F1)):
        slot = 2 * b_f + h
        arrived(dv.at[slot], sa_r.at[role])
        relay(dv.at[slot], dv.at[slot], (FZ0, FZ1)[h], b_z)
    for slot in (2 * b_m, 2 * b_p + 1, 2 * b_z, 2 * b_z + 1, 2 * b_f, 2 * b_f + 1):
        accumulate(slot)
    next(table_gather)
    for slot, roles in ((2 * b_m + 1, (M1A, M1B)), (2 * b_p, (P0A, P0B))):
        for r in range(2):
            arrived(dv.at[slot, pl.ds(r * 128, 128)], sa_r.at[roles[r]])
        accumulate(slot)
    for slot, role in ((2 * b_mz, MZ0), (2 * b_pz, PZ0)):
        arrived(dv.at[slot], sa_r.at[role])
        accumulate(slot)
    next(table_gather)
    for slot, role in ((2 * b_fz, FZ0), (2 * b_mz + 1, MZ1), (2 * b_pz + 1, PZ1), (2 * b_fz + 1, FZ1)):
        arrived(dv.at[slot], sa_r.at[role])
        accumulate(slot)

    applied = acc[...].astype(BF)
    raw = jnp.zeros((256, 256), F32)
    for h in range(2):
        raw += lax.dot_general(
            dv[2 * b + h], applied[h * 256 : h * 256 + 256], (((0,), (0,)), ((), ())), preferred_element_type=F32
        )
    kp[...] = (0.5 * (raw + raw.T)).astype(BF).reshape(8, 32, 256)
    for j, dest in enumerate(pw_out):
        pending.append(send(kp.at[dest], kr.at[b], sk_s.at[j], sk_r.at[j], pw=dest))
    kr[b] = kp[b]

    next(table_gather)
    next(table_gather)
    t2f[...] = t2[...].reshape(1024, 128).astype(F32)

    def coefficients(i, carry):
        for h in range(2):
            this = (2 * i + h).astype(F32)
            total = jnp.zeros((128, 128), F32)
            for j in range(4):
                index = t2f[pl.ds(j, 128, stride=8), :]
                weight = t2f[pl.ds(4 + j, 128, stride=8), :]
                total += jnp.where(index == this, weight, 0.0)
            ct[i, :, h * 128 : h * 128 + 128] = total.astype(BF)
        return carry

    lax.fori_loop(0, 16, coefficients, 0)

    for j, source in enumerate(pw_in):
        arrived(kr.at[source], sk_r.at[j])
    total = kr[0].astype(F32)
    for j in range(1, 8):
        total += kr[j].astype(F32)
    kt[x, zh, core] = total.astype(BF)
    kernel_gather = gather(kt, 1)
    next(kernel_gather)

    def mix(app):
        for j, source in enumerate(pw_in):
            arrived(yrecv.at[app, source], sy_r.at[app, j])
        columns = yrecv[app].reshape(128, 128).astype(F32).T.astype(BF)

        def step(i, carry):
            mixed = dot(columns, ct[i]).astype(BF)
            for h in range(2):
                for n in range(4):
                    ucat[2 * i + h, :, n * 128 : n * 128 + 128] = mixed[
                        n * 32 : n * 32 + 32, h * 128 : h * 128 + 128
                    ]
            return carry

        lax.fori_loop(0, 16, step, 0, unroll=2)

    def contract(app):
        product = dot(kcat[...], ucat[...].reshape(1024, 512))
        zs[app] = product.T.astype(BF).reshape(4, 128, 256)
        part = pl.ds(pl.multiple_of(b * 16, 16), 16)
        zr[app, b] = zs[app, :, part, :]
        for j, dest in enumerate(pw_out):
            part = pl.ds(pl.multiple_of(dest * 16, 16), 16)
            pending.append(send(zs.at[app, :, part, :], zr.at[app, b], sz_s.at[app, j], sz_r.at[app, j], pw=dest))

    def summed(app):
        for j, source in enumerate(pw_in):
            arrived(zr.at[app, source], sz_r.at[app, j])
        rows = zr[app, 0].astype(F32)
        for j in range(1, 8):
            rows += zr[app, j].astype(F32)
        return rows.reshape(64, 256)

    norm_scale = 1.0 / math.sqrt(32768.0)
    def finish(app, vector):
        return norm_scale * live * transforms(summed(app), False) + energy * vector

    mix(0)
    for _ in kernel_gather:
        pass
    for i in range(8):
        rows = kt[i // 2, 2 * (i % 2) : 2 * (i % 2) + 2].reshape(128, 256)
        kcat[:, i * 128 : i * 128 + 128] = rows.astype(F32).T.astype(BF)
    contract(0)
    first = finish(0, rows_x[...]).astype(BF)
    first_wide = first.astype(F32)
    spread_columns(1, transforms(live * first_wide, True))

    r_in, r_out = iota((64, 64), 1), iota((64, 64), 0)
    order = (r_in == ((r_out // 4) % 4) * 16 + (r_out // 16) * 4 + r_out % 4).astype(F32).astype(BF)
    fs[...] = dot(order, first).astype(BF).reshape(4, 16, 256)
    first_sends = []
    for i in range(4):
        target = 4 * b + i

        @pl.when(target == a)
        def _():
            fb[a] = fs[i]

        @pl.when(target != a)
        def _():
            send(fs.at[i], fb.at[a], sf_s.at[i], sf_r.at[a], pair=target)

    mix(1)
    contract(1)

    root = a // 4
    d_y = (y + 4 - root // 2) % 4
    d_z = (zl + root % 2) % 2
    is_root = (d_y == 0) & (d_z == 0)
    odd = d_y % 2 == 1

    @pl.when(b == root)
    def _():
        def take(s, carry):
            @pl.when(s != a)
            def _():
                arrived(fb.at[s], sf_r.at[s])

            return carry

        lax.fori_loop(0, 32, take, 0)
        wide = fb[...].reshape(512, 256).astype(F32)
        for u in range(2):
            fbf[u] = wide[:, u * 128 : u * 128 + 128]
        for k in range(4):
            for u in range(2):
                at = k * 256 + u * 128
                out1[at : at + 128, :] = fbf[u, pl.ds(k, 128, stride=4), :].T.astype(BF)

    def half(h):
        return out1.at[pl.ds(h * 512, 512)]

    def pass_on(h, pw, slot):
        return pltpu.make_async_remote_copy(
            src_ref=half(h), dst_ref=half(h), send_sem=sb_s.at[slot], recv_sem=sb_r.at[h],
            device_id={"pair": a, "pw": pw}, device_id_type=MESH,
        )

    to_p = [pass_on(h, b_p, h) for h in range(2)]
    to_m = [pass_on(h, b_m, 2 + h) for h in range(2)]
    to_z = [pass_on(h, b_z, 4 + h) for h in range(2)]

    def take_halves():
        for h in range(2):
            arrived(half(h), sb_r.at[h])

    @pl.when(is_root)
    def _():
        for h in range(2):
            to_z[h].start()
            to_p[h].start()
            to_m[h].start()

    second = 2.0 * finish(1, first_wide) - rows_x[...]
    g[x, zh, core] = second.astype(BF)
    last_gather = gather(g, 2)
    next(last_gather)
    next(last_gather)

    @pl.when((d_y == 0) & (d_z == 1))
    def _():
        take_halves()
        for h in range(2):
            to_p[h].start()
            to_m[h].start()

    @pl.when(odd & (d_z == 0))
    def _():
        take_halves()

    @pl.when((d_y == 1) & (d_z == 0))
    def _():
        to_p[0].start()

    @pl.when((d_y == 3) & (d_z == 0))
    def _():
        to_m[1].start()

    next(last_gather)
    next(last_gather)

    @pl.when(odd & (d_z == 1))
    def _():
        take_halves()

    @pl.when((d_y == 1) & (d_z == 1))
    def _():
        to_p[0].start()

    @pl.when((d_y == 3) & (d_z == 1))
    def _():
        to_m[1].start()

    next(last_gather)

    @pl.when(d_y == 2)
    def _():
        take_halves()

    for copy in pending:
        copy.wait_send()
    for i in range(4):
        target = 4 * b + i

        @pl.when(target != a)
        def _():
            pltpu.make_async_copy(fs.at[i], fs.at[i], sf_s.at[i]).wait()

    @pl.when(is_root)
    def _():
        for h in range(2):
            to_z[h].wait_send()

    @pl.when(d_y == 0)
    def _():
        for h in range(2):
            to_p[h].wait_send()
            to_m[h].wait_send()

    @pl.when(d_y == 1)
    def _():
        to_p[0].wait_send()

    @pl.when(d_y == 3)
    def _():
        to_m[1].wait_send()


def layout(first_ref, g_ref, out1, out2, wide, stage, sem):
    copies = [pltpu.make_async_copy(first_ref, out1, sem.at[4])]
    copies[0].start()
    rows = g_ref[...].reshape(2048, 256).astype(F32)
    for u in range(2):
        wide[u] = rows[:, u * 128 : u * 128 + 128]
    for i in range(4):
        for k in range(4 * i, 4 * i + 4):
            for u in range(2):
                at = k * 256 + u * 128
                stage[at : at + 128, :] = wide[u, pl.ds(k, 128, stride=16), :].T
        part = pl.ds(i * 1024, 1024)
        copies.append(pltpu.make_async_copy(stage.at[part], out2.at[part], sem.at[i]))
        copies[-1].start()
    for copy in copies:
        copy.wait()


def shards(screened, density, transform, energy, trial, coarse_index, interp_weight, bands):
    hbm = pl.BlockSpec(memory_space=pltpu.HBM)
    vmem = pl.BlockSpec(memory_space=pltpu.VMEM)
    dma = pltpu.SemaphoreType.DMA
    first, gathered = pl.pallas_call(
        kernel,
        out_shape=(jax.ShapeDtypeStruct((1024, 128), BF), jax.ShapeDtypeStruct((4, 4, 2, 64, 256), BF)),
        in_specs=[hbm] * 8,
        out_specs=(vmem, vmem),
        scratch_shapes=[
            pltpu.VMEM((512, 4096), BF),
            pltpu.VMEM((16, 256, 256), BF),
            pltpu.VMEM((16, 256, 256), BF),
            pltpu.VMEM((4096, 128), BF),
            pltpu.VMEM((512, 256), F32),
            pltpu.VMEM((8, 32, 256), BF),
            pltpu.VMEM((8, 32, 256), BF),
            pltpu.VMEM((4, 4, 2, 32, 256), BF),
            pltpu.VMEM((256, 1024), BF),
            pltpu.VMEM((4, 8, 128), F32),
            pltpu.VMEM((8, 32, 128), BF),
            pltpu.VMEM((4, 4, 2, 32, 128), BF),
            pltpu.VMEM((1024, 128), F32),
            pltpu.VMEM((16, 128, 256), BF),
            pltpu.VMEM((32, 32, 512), BF),
            pltpu.VMEM((2, 8, 16, 128), BF),
            pltpu.VMEM((2, 8, 16, 128), BF),
            pltpu.VMEM((2, 4, 128, 256), BF),
            pltpu.VMEM((2, 8, 4, 16, 256), BF),
            pltpu.VMEM((64, 256), F32),
            pltpu.VMEM((4, 16, 256), BF),
            pltpu.VMEM((32, 16, 256), BF),
            pltpu.VMEM((2, 512, 128), F32),
            pltpu.VMEM((1, 128), jnp.int32),
            pltpu.VMEM((32, 128), F32),
            pltpu.VMEM((4, 4, 16), jnp.int32),
            pltpu.VMEM((4, 4, 16), BF),
            dma((12,)),
            dma((16,)), dma((16,)),
            dma((6,)), dma((2,)),
            dma((2, 7)), dma((2, 7)),
            dma((7,)), dma((7,)),
            dma((2, 7)), dma((2, 7)),
            dma((7,)), dma((7,)),
            dma((3, 19)), dma((3, 19)),
            dma((4,)), dma((32,)),
        ],
        compiler_params=pltpu.CompilerParams(
            collective_id=0, has_side_effects=True, vmem_limit_bytes=48 * 1024 * 1024
        ),
        name="bse_chebyshev",
    )(
        *[
            pltpu.with_memory_space_constraint(value, pltpu.HBM)
            for value in (
                screened, density, transform, trial, bands.reshape(1, 128), energy.reshape(32, 128),
                jnp.transpose(coarse_index, (0, 2, 1)), jnp.transpose(interp_weight, (0, 2, 1)),
            )
        ]
    )
    return pl.pallas_call(
        layout,
        out_shape=(jax.ShapeDtypeStruct((1024, 128), BF), jax.ShapeDtypeStruct((4096, 128), F32)),
        in_specs=[vmem] * 2,
        out_specs=(hbm, hbm),
        scratch_shapes=[pltpu.VMEM((2, 2048, 128), F32), pltpu.VMEM((4096, 128), F32), dma((5,))],
        compiler_params=pltpu.CompilerParams(vmem_limit_bytes=48 * 1024 * 1024),
        name="layout",
    )(first, gathered)


def solution(mesh):
    in_specs = (
        P("pair", "pw", None),
        P("pair", "pw", None),
        P("pw", None, None),
        P("pw"),
        P("pw", None),
        P("pair", "pw", None),
        P("pair", "pw", None),
        P(),
    )
    out_specs = (P("pair", None), P("pw", None))
    return jax.shard_map(shards, mesh=mesh, in_specs=in_specs, out_specs=out_specs, check_vma=False)
```

```python
import math

import jax
import jax.numpy as jnp
from jax import lax
from jax.experimental import pallas as pl
from jax.experimental.pallas import tpu as pltpu
from jax.sharding import PartitionSpec as P

MESH = pl.DeviceIdType.MESH
BF = jnp.bfloat16
F32 = jnp.float32
NCOND = 16


def dot(lhs, rhs):
    return jnp.dot(lhs, rhs, preferred_element_type=F32)


def dot_t(lhs, rhs):
    return lax.dot_general(lhs, rhs, (((1,), (1,)), ((), ())), preferred_element_type=F32)


def iota(shape, dim):
    return lax.broadcasted_iota(jnp.int32, shape, dim)


def kernel(
    w_hbm, d_hbm, t_hbm, x_hbm, bands_hbm, energy_hbm, index_hbm, weight_hbm,
    out1, g,
    wv, dv, tv, xv, acc, kp, kr, kt, kcat, tab, tb, t2, t2f, ct, ucat, ysend, yrecv, zs, zr,
    rows_x, fs, fb, fbf, bands_ref, energy_ref, index_ref, weight_ref,
    rounds, sem_local, sa_s, sa_r, sb_s, sb_r, sy_s, sy_r, sk_s, sk_r, sz_s, sz_r, sq_s, sq_r,
    sg_s, sg_r, sf_s, sf_r,
):
    a = lax.axis_index("pair")
    b = lax.axis_index("pw")
    x, zh, core = a // 8, (a // 2) % 4, a % 2
    y, zl = b // 2, b % 2
    b_p = ((y + 1) % 4) * 2 + zl
    b_m = ((y + 3) % 4) * 2 + zl
    b_f = ((y + 2) % 4) * 2 + zl
    b_z = y * 2 + 1 - zl
    b_pz = ((y + 1) % 4) * 2 + 1 - zl
    b_mz = ((y + 3) % 4) * 2 + 1 - zl
    b_fz = ((y + 2) % 4) * 2 + 1 - zl
    pw_out = (b_fz, b_f, b_pz, b_mz, b_p, b_m, b_z)
    pw_in = (b_fz, b_f, b_mz, b_pz, b_m, b_p, b_z)
    pending = []

    pair_c = x * 8 + zh * 2 + 1 - core

    def send(src, dst, s_sem, r_sem, pair=None, pw=None):
        copy = pltpu.make_async_remote_copy(
            src_ref=src, dst_ref=dst, send_sem=s_sem, recv_sem=r_sem,
            device_id={"pair": a if pair is None else pair, "pw": b if pw is None else pw},
            device_id_type=MESH,
        )
        copy.start()
        return copy

    def arrived(slot, sem):
        pltpu.make_async_copy(slot, slot, sem).wait()

    barrier = pltpu.get_barrier_semaphore()
    z_other = (zh + 3 + 2 * zl) % 4
    peers = [(a, b_p), (a, b_m), (a, b_z), (x * 8 + z_other * 2 + core, b_z), (pair_c, b)]
    peers += [(((x + j) % 4) * 8 + zh * 2 + core, b) for j in (1, 3)]

    def greet(sem):
        for pair, pw in peers:
            pl.semaphore_signal(sem, inc=1, device_id={"pair": pair, "pw": pw}, device_id_type=MESH)

    greet(barrier)
    x_load = pltpu.make_async_copy(x_hbm, xv, sem_local.at[0])
    t_load = pltpu.make_async_copy(t_hbm, tv, sem_local.at[1])
    d_loads = [
        pltpu.make_async_copy(d_hbm.at[0, pl.ds(h * 256, 256)], dv.at[2 * b + h], sem_local.at[2 + h]) for h in range(2)
    ]
    w_loads = [
        pltpu.make_async_copy(w_hbm.at[0, pl.ds(i * 128, 128)], wv.at[pl.ds(i * 128, 128)], sem_local.at[4 + i])
        for i in range(4)
    ]
    for load in d_loads:
        load.start()
    x_load.start()
    small_loads = [
        pltpu.make_async_copy(src, dst, sem_local.at[8 + i])
        for i, (src, dst) in enumerate((
            (index_hbm, index_ref), (weight_hbm, weight_ref), (bands_hbm, bands_ref), (energy_hbm, energy_ref)
        ))
    ]
    for load in [*small_loads, t_load, *w_loads]:
        load.start()
    for load in d_loads:
        load.wait()
    pl.semaphore_wait(barrier, len(peers))
    greet(rounds.at[0])

    M0, M1A, M1B, F0, MZ0, MZ1, P1, P0A, P0B, F1, PZ0, PZ1, Z0, Z1, FZ0, FZ1 = range(16)
    sent = [0]

    def relay(src, dst, role, pw):
        pending.append(send(src, dst, sa_s.at[sent[0]], sa_r.at[role], pw=pw))
        sent[0] += 1

    def quarter(h, r):
        return dv.at[2 * b + h, pl.ds(r * 128, 128)]

    own = [dv.at[2 * b + h] for h in range(2)]
    quarters = [[quarter(h, r) for r in range(2)] for h in range(2)]
    relay(own[0], dv.at[2 * b], M0, b_p)
    relay(own[1], dv.at[2 * b + 1], P1, b_m)
    relay(own[0], dv.at[2 * b], Z0, b_z)
    relay(quarters[1][0], quarter(1, 0), M1A, b_p)
    relay(quarters[0][0], quarter(0, 0), P0A, b_m)
    relay(own[1], dv.at[2 * b + 1], Z1, b_z)

    for load in small_loads:
        load.wait()

    tab[...] = jnp.zeros_like(tab)
    tab[:, 0:4, 0:16] = index_ref[...].astype(F32)
    tab[:, 4:8, 0:16] = weight_ref[...].astype(F32)
    tb[b] = tab[...].reshape(32, 128).astype(BF)
    own_bands = jnp.where(iota((16, 128), 1) == 16 * b + iota((16, 128), 0), bands_ref[...].astype(F32), 0.0)
    own_bands = jnp.sum(own_bands, axis=1, keepdims=True)
    live = ((iota((16, 256), 1) % NCOND).astype(F32) < own_bands).astype(F32)
    live = jnp.concatenate([live] * 4, axis=0)
    energy = jnp.concatenate([energy_ref[pl.ds(u, 16, stride=2), :] for u in range(2)], axis=1)
    energy = jnp.concatenate([energy] * 4, axis=0)
    chosen = (iota((8, 128), 1) == 4 * a + iota((8, 128), 0)) & (iota((8, 128), 0) < 4)
    chosen = chosen.astype(F32).astype(BF)
    x_load.wait()
    for k in range(16):
        picked = dot_t(chosen, xv[k * 256 : (k + 1) * 256, :])
        for n in range(4):
            rows_x[n * 16 + k : n * 16 + k + 1, :] = picked[n : n + 1, :]
    for i in range(2):
        pl.semaphore_wait(rounds.at[i], len(peers))
        greet(rounds.at[i + 1])
    for j, dest in enumerate(pw_out):
        pending.append(send(tb.at[b], tb.at[b], sq_s.at[j], sq_r.at[j], pw=dest))

    z_of = (zh, (zh + 1) % 4, (zh + 3) % 4, (zh + 2) % 4)
    x_of = (x, (x + 1) % 4, (x + 3) % 4, (x + 2) % 4)
    from_of = (0, 2, 1, 3)

    def gather(buf, n):
        def move(part, index, pair):
            pending.append(send(part, part, sg_s.at[n, index], sg_r.at[n, index], pair=pair))

        def x_out(p):
            for i in (3, 1, 2):
                move(buf.at[x, z_of[p], core], 3 * p + i + 2, x_of[i] * 8 + zh * 2 + core)

        def x_in(p):
            for i in (1, 2, 3):
                arrived(buf.at[x_of[i], z_of[p], core], sg_r.at[n, 3 * p + from_of[i] + 2])
            move(buf.at[:, z_of[p], core], 15 + p, pair_c)

        def z_in(i):
            arrived(buf.at[x, z_of[i], core], sg_r.at[n, from_of[i] - 1])
            x_out(i)

        for i in (3, 1, 2):
            move(buf.at[x, zh, core], i - 1, x * 8 + z_of[i] * 2 + core)
        x_out(0)
        yield
        z_in(1)
        z_in(2)
        yield
        z_in(3)
        x_in(0)
        yield
        x_in(1)
        x_in(2)
        x_in(3)
        yield
        for p in range(4):
            arrived(buf.at[:, z_of[p], 1 - core], sg_r.at[n, 15 + p])
        yield

    row_k = iota((64, 256), 0) % 16
    lane = iota((16, 128), 1)

    def transforms(rows, transposed):
        def step(k, total):
            mine = jnp.where(row_k == k, rows, 0.0).astype(BF)
            return total + (dot_t if transposed else dot)(mine, tv[k])

        return lax.fori_loop(0, 16, step, jnp.zeros((64, 256), F32), unroll=16)

    def spread_columns(app, rows):
        for part in range(8):
            i, half = part % 4, part // 4
            block = jnp.zeros((16, 128), F32)
            for n in range(4):
                piece = rows[n * 16 : n * 16 + 16, half * 128 : half * 128 + 128]
                shift = ((n - i) * 32) % 128
                if shift:
                    piece = pltpu.roll(piece, shift, axis=1)
                block = jnp.where(lane // 32 == n, piece, block)
            ysend[app, part] = block.astype(BF)
        yrecv[app, b] = ysend[app, b]
        for j, dest in enumerate(pw_out):
            pending.append(send(ysend.at[app, dest], yrecv.at[app, b], sy_s.at[app, j], sy_r.at[app, j], pw=dest))

    t_load.wait()
    spread_columns(0, transforms(live * rows_x[...], True))

    def accumulate(slot, first=False):
        columns = pl.ds(pl.multiple_of(slot * 256, 256), 256)
        product = dot(wv[:, columns], dv[slot])
        if first:
            acc[...] = product
        else:
            acc[...] += product

    arrived(dv.at[2 * b_m], sa_r.at[M0])
    relay(dv.at[2 * b_m], dv.at[2 * b_m], F0, b_p)
    relay(quarters[1][1], quarter(1, 1), M1B, b_p)
    arrived(dv.at[2 * b_p + 1], sa_r.at[P1])
    relay(dv.at[2 * b_p + 1], dv.at[2 * b_p + 1], F1, b_m)
    relay(quarters[0][1], quarter(0, 1), P0B, b_m)

    table_lane = iota((32, 128), 1) // 16
    table_rows = jnp.zeros((32, 128), F32)
    for j, source in enumerate(pw_in):
        arrived(tb.at[source], sq_r.at[j])
    for s in range(8):
        piece = tb[s].astype(F32)
        if s:
            piece = pltpu.roll(piece, 16 * s, axis=1)
        table_rows = jnp.where(table_lane == s, piece, table_rows)
    t2[x, zh, core] = table_rows.astype(BF)
    pl.semaphore_wait(rounds.at[2], len(peers))
    table_gather = gather(t2, 0)
    next(table_gather)

    for h, role in ((0, Z0), (1, Z1)):
        slot = 2 * b_z + h
        arrived(dv.at[slot], sa_r.at[role])
        relay(dv.at[slot], dv.at[slot], (MZ0, MZ1)[h], b_p)
        relay(dv.at[slot], dv.at[slot], (PZ0, PZ1)[h], b_m)
    for load in w_loads:
        load.wait()
    accumulate(2 * b, True)
    accumulate(2 * b + 1)
    for h, role in ((0, F0), (1, F1)):
        slot = 2 * b_f + h
        arrived(dv.at[slot], sa_r.at[role])
        relay(dv.at[slot], dv.at[slot], (FZ0, FZ1)[h], b_z)
    for slot in (2 * b_m, 2 * b_p + 1, 2 * b_z, 2 * b_z + 1, 2 * b_f, 2 * b_f + 1):
        accumulate(slot)
    next(table_gather)
    for slot, roles in ((2 * b_m + 1, (M1A, M1B)), (2 * b_p, (P0A, P0B))):
        for r in range(2):
            arrived(dv.at[slot, pl.ds(r * 128, 128)], sa_r.at[roles[r]])
        accumulate(slot)
    for slot, role in ((2 * b_mz, MZ0), (2 * b_pz, PZ0)):
        arrived(dv.at[slot], sa_r.at[role])
        accumulate(slot)
    next(table_gather)
    for slot, role in ((2 * b_fz, FZ0), (2 * b_mz + 1, MZ1), (2 * b_pz + 1, PZ1), (2 * b_fz + 1, FZ1)):
        arrived(dv.at[slot], sa_r.at[role])
        accumulate(slot)

    applied = acc[...].astype(BF)
    raw = jnp.zeros((256, 256), F32)
    for h in range(2):
        raw += lax.dot_general(
            dv[2 * b + h], applied[h * 256 : h * 256 + 256], (((0,), (0,)), ((), ())), preferred_element_type=F32
        )
    kp[...] = (0.5 * (raw + raw.T)).astype(BF).reshape(8, 32, 256)
    for j, dest in enumerate(pw_out):
        pending.append(send(kp.at[dest], kr.at[b], sk_s.at[j], sk_r.at[j], pw=dest))
    kr[b] = kp[b]

    next(table_gather)
    next(table_gather)
    t2f[...] = t2[...].reshape(1024, 128).astype(F32)

    def coefficients(i, carry):
        for h in range(2):
            this = (2 * i + h).astype(F32)
            total = jnp.zeros((128, 128), F32)
            for j in range(4):
                index = t2f[pl.ds(j, 128, stride=8), :]
                weight = t2f[pl.ds(4 + j, 128, stride=8), :]
                total += jnp.where(index == this, weight, 0.0)
            ct[i, :, h * 128 : h * 128 + 128] = total.astype(BF)
        return carry

    lax.fori_loop(0, 16, coefficients, 0)

    for j, source in enumerate(pw_in):
        arrived(kr.at[source], sk_r.at[j])
    total = kr[0].astype(F32)
    for j in range(1, 8):
        total += kr[j].astype(F32)
    kt[x, zh, core] = total.astype(BF)
    kernel_gather = gather(kt, 1)
    next(kernel_gather)

    def mix(app):
        for j, source in enumerate(pw_in):
            arrived(yrecv.at[app, source], sy_r.at[app, j])
        columns = yrecv[app].reshape(128, 128).astype(F32).T.astype(BF)

        def step(i, carry):
            mixed = dot(columns, ct[i]).astype(BF)
            for h in range(2):
                for n in range(4):
                    ucat[2 * i + h, :, n * 128 : n * 128 + 128] = mixed[
                        n * 32 : n * 32 + 32, h * 128 : h * 128 + 128
                    ]
            return carry

        lax.fori_loop(0, 16, step, 0, unroll=8)

    def contract(app):
        product = dot(kcat[...], ucat[...].reshape(1024, 512))
        zs[app] = product.T.astype(BF).reshape(4, 128, 256)
        part = pl.ds(pl.multiple_of(b * 16, 16), 16)
        zr[app, b] = zs[app, :, part, :]
        for j, dest in enumerate(pw_out):
            part = pl.ds(pl.multiple_of(dest * 16, 16), 16)
            pending.append(send(zs.at[app, :, part, :], zr.at[app, b], sz_s.at[app, j], sz_r.at[app, j], pw=dest))

    def summed(app):
        for j, source in enumerate(pw_in):
            arrived(zr.at[app, source], sz_r.at[app, j])
        rows = zr[app, 0].astype(F32)
        for j in range(1, 8):
            rows += zr[app, j].astype(F32)
        return rows.reshape(64, 256)

    norm_scale = 1.0 / math.sqrt(32768.0)
    def finish(app, vector):
        return norm_scale * live * transforms(summed(app), False) + energy * vector

    mix(0)
    for _ in kernel_gather:
        pass
    for i in range(8):
        rows = kt[i // 2, 2 * (i % 2) : 2 * (i % 2) + 2].reshape(128, 256)
        kcat[:, i * 128 : i * 128 + 128] = rows.astype(F32).T.astype(BF)
    contract(0)
    first = finish(0, rows_x[...]).astype(BF)
    first_wide = first.astype(F32)
    spread_columns(1, transforms(live * first_wide, True))

    r_in, r_out = iota((64, 64), 1), iota((64, 64), 0)
    order = (r_in == ((r_out // 4) % 4) * 16 + (r_out // 16) * 4 + r_out % 4).astype(F32).astype(BF)
    fs[...] = dot(order, first).astype(BF).reshape(4, 16, 256)
    first_sends = []
    for i in range(4):
        target = 4 * b + i

        @pl.when(target == a)
        def _():
            fb[a] = fs[i]

        @pl.when(target != a)
        def _():
            send(fs.at[i], fb.at[a], sf_s.at[i], sf_r.at[a], pair=target)

    mix(1)
    contract(1)

    root = a // 4
    d_y = (y + 4 - root // 2) % 4
    d_z = (zl + root % 2) % 2
    is_root = (d_y == 0) & (d_z == 0)
    odd = d_y % 2 == 1

    @pl.when(b == root)
    def _():
        def take(s, carry):
            @pl.when(s != a)
            def _():
                arrived(fb.at[s], sf_r.at[s])

            return carry

        lax.fori_loop(0, 32, take, 0)
        wide = fb[...].reshape(512, 256).astype(F32)
        for u in range(2):
            fbf[u] = wide[:, u * 128 : u * 128 + 128]
        for k in range(4):
            for u in range(2):
                at = k * 256 + u * 128
                out1[at : at + 128, :] = fbf[u, pl.ds(k, 128, stride=4), :].T.astype(BF)

    def half(h):
        return out1.at[pl.ds(h * 512, 512)]

    def pass_on(h, pw, slot):
        return pltpu.make_async_remote_copy(
            src_ref=half(h), dst_ref=half(h), send_sem=sb_s.at[slot], recv_sem=sb_r.at[h],
            device_id={"pair": a, "pw": pw}, device_id_type=MESH,
        )

    to_p = [pass_on(h, b_p, h) for h in range(2)]
    to_m = [pass_on(h, b_m, 2 + h) for h in range(2)]
    to_z = [pass_on(h, b_z, 4 + h) for h in range(2)]

    def take_halves():
        for h in range(2):
            arrived(half(h), sb_r.at[h])

    @pl.when(is_root)
    def _():
        to_z[0].start()
        for h in range(2):
            to_p[h].start()
            to_m[h].start()

    second = 2.0 * finish(1, first_wide) - rows_x[...]
    g[x, zh, core] = second.astype(BF)
    last_gather = gather(g, 2)
    next(last_gather)

    @pl.when(is_root)
    def _():
        to_z[1].start()

    next(last_gather)

    @pl.when((d_y == 0) & (d_z == 1))
    def _():
        arrived(half(0), sb_r.at[0])
        to_p[0].start()
        to_m[0].start()

    @pl.when(odd & (d_z == 0))
    def _():
        take_halves()

    @pl.when((d_y == 1) & (d_z == 0))
    def _():
        to_p[0].start()

    @pl.when((d_y == 3) & (d_z == 0))
    def _():
        to_m[1].start()

    next(last_gather)

    @pl.when((d_y == 0) & (d_z == 1))
    def _():
        arrived(half(1), sb_r.at[1])
        to_p[1].start()
        to_m[1].start()

    next(last_gather)

    @pl.when(odd & (d_z == 1))
    def _():
        take_halves()

    @pl.when((d_y == 1) & (d_z == 1))
    def _():
        to_p[0].start()

    @pl.when((d_y == 3) & (d_z == 1))
    def _():
        to_m[1].start()

    next(last_gather)

    @pl.when(d_y == 2)
    def _():
        take_halves()

    for copy in pending:
        copy.wait_send()
    for i in range(4):
        target = 4 * b + i

        @pl.when(target != a)
        def _():
            pltpu.make_async_copy(fs.at[i], fs.at[i], sf_s.at[i]).wait()

    @pl.when(is_root)
    def _():
        for h in range(2):
            to_z[h].wait_send()

    @pl.when(d_y == 0)
    def _():
        for h in range(2):
            to_p[h].wait_send()
            to_m[h].wait_send()

    @pl.when(d_y == 1)
    def _():
        to_p[0].wait_send()

    @pl.when(d_y == 3)
    def _():
        to_m[1].wait_send()


def layout(first_ref, g_ref, out1, out2, wide, stage, sem):
    copies = [pltpu.make_async_copy(first_ref, out1, sem.at[4])]
    copies[0].start()
    rows = g_ref[...].reshape(2048, 256).astype(F32)
    for u in range(2):
        wide[u] = rows[:, u * 128 : u * 128 + 128]
    for i in range(4):
        for k in range(4 * i, 4 * i + 4):
            for u in range(2):
                at = k * 256 + u * 128
                stage[at : at + 128, :] = wide[u, pl.ds(k, 128, stride=16), :].T
        part = pl.ds(i * 1024, 1024)
        copies.append(pltpu.make_async_copy(stage.at[part], out2.at[part], sem.at[i]))
        copies[-1].start()
    for copy in copies:
        copy.wait()


def shards(screened, density, transform, energy, trial, coarse_index, interp_weight, bands):
    hbm = pl.BlockSpec(memory_space=pltpu.HBM)
    vmem = pl.BlockSpec(memory_space=pltpu.VMEM)
    dma = pltpu.SemaphoreType.DMA
    first, gathered = pl.pallas_call(
        kernel,
        out_shape=(jax.ShapeDtypeStruct((1024, 128), BF), jax.ShapeDtypeStruct((4, 4, 2, 64, 256), BF)),
        in_specs=[hbm] * 8,
        out_specs=(vmem, vmem),
        scratch_shapes=[
            pltpu.VMEM((512, 4096), BF),
            pltpu.VMEM((16, 256, 256), BF),
            pltpu.VMEM((16, 256, 256), BF),
            pltpu.VMEM((4096, 128), BF),
            pltpu.VMEM((512, 256), F32),
            pltpu.VMEM((8, 32, 256), BF),
            pltpu.VMEM((8, 32, 256), BF),
            pltpu.VMEM((4, 4, 2, 32, 256), BF),
            pltpu.VMEM((256, 1024), BF),
            pltpu.VMEM((4, 8, 128), F32),
            pltpu.VMEM((8, 32, 128), BF),
            pltpu.VMEM((4, 4, 2, 32, 128), BF),
            pltpu.VMEM((1024, 128), F32),
            pltpu.VMEM((16, 128, 256), BF),
            pltpu.VMEM((32, 32, 512), BF),
            pltpu.VMEM((2, 8, 16, 128), BF),
            pltpu.VMEM((2, 8, 16, 128), BF),
            pltpu.VMEM((2, 4, 128, 256), BF),
            pltpu.VMEM((2, 8, 4, 16, 256), BF),
            pltpu.VMEM((64, 256), F32),
            pltpu.VMEM((4, 16, 256), BF),
            pltpu.VMEM((32, 16, 256), BF),
            pltpu.VMEM((2, 512, 128), F32),
            pltpu.VMEM((1, 128), jnp.int32),
            pltpu.VMEM((32, 128), F32),
            pltpu.VMEM((4, 4, 16), jnp.int32),
            pltpu.VMEM((4, 4, 16), BF),
            pltpu.SemaphoreType.REGULAR((3,)),
            dma((12,)),
            dma((16,)), dma((16,)),
            dma((6,)), dma((2,)),
            dma((2, 7)), dma((2, 7)),
            dma((7,)), dma((7,)),
            dma((2, 7)), dma((2, 7)),
            dma((7,)), dma((7,)),
            dma((3, 19)), dma((3, 19)),
            dma((4,)), dma((32,)),
        ],
        compiler_params=pltpu.CompilerParams(
            collective_id=0, has_side_effects=True, vmem_limit_bytes=48 * 1024 * 1024
        ),
        name="bse_chebyshev",
    )(
        *[
            pltpu.with_memory_space_constraint(value, pltpu.HBM)
            for value in (
                screened, density, transform, trial, bands.reshape(1, 128), energy.reshape(32, 128),
                jnp.transpose(coarse_index, (0, 2, 1)), jnp.transpose(interp_weight, (0, 2, 1)),
            )
        ]
    )
    return pl.pallas_call(
        layout,
        out_shape=(jax.ShapeDtypeStruct((1024, 128), BF), jax.ShapeDtypeStruct((4096, 128), F32)),
        in_specs=[vmem] * 2,
        out_specs=(hbm, hbm),
        scratch_shapes=[pltpu.VMEM((2, 2048, 128), F32), pltpu.VMEM((4096, 128), F32), dma((5,))],
        compiler_params=pltpu.CompilerParams(vmem_limit_bytes=48 * 1024 * 1024),
        name="layout",
    )(first, gathered)


def solution(mesh):
    in_specs = (
        P("pair", "pw", None),
        P("pair", "pw", None),
        P("pw", None, None),
        P("pw"),
        P("pw", None),
        P("pair", "pw", None),
        P("pair", "pw", None),
        P(),
    )
    out_specs = (P("pair", None), P("pw", None))
    return jax.shard_map(shards, mesh=mesh, in_specs=in_specs, out_specs=out_specs, check_vma=False)
```

```python
import math

import jax
import jax.numpy as jnp
from jax import lax
from jax.experimental import pallas as pl
from jax.experimental.pallas import tpu as pltpu
from jax.sharding import PartitionSpec as P

MESH = pl.DeviceIdType.MESH
BF = jnp.bfloat16
F32 = jnp.float32
NCOND = 16


def dot(lhs, rhs):
    return jnp.dot(lhs, rhs, preferred_element_type=F32)


def dot_t(lhs, rhs):
    return lax.dot_general(lhs, rhs, (((1,), (1,)), ((), ())), preferred_element_type=F32)


def iota(shape, dim):
    return lax.broadcasted_iota(jnp.int32, shape, dim)


def kernel(
    w_hbm, d_hbm, t_hbm, x_hbm, bands_hbm, energy_hbm, index_hbm, weight_hbm,
    out1, g,
    wv, dv, tv, xv, acc, kp, kr, kt, kcat, tab, tb, t2, t2f, ct, ucat, ysend, yrecv, zs, zr,
    rows_x, fs, fb, fbf, bands_ref, energy_ref, index_ref, weight_ref,
    rounds, sem_local, sa_s, sa_r, sb_s, sb_r, sy_s, sy_r, sk_s, sk_r, sz_s, sz_r, sq_s, sq_r,
    sg_s, sg_r, sf_s, sf_r,
):
    a = lax.axis_index("pair")
    b = lax.axis_index("pw")
    x, zh, core = a // 8, (a // 2) % 4, a % 2
    y, zl = b // 2, b % 2
    b_p = ((y + 1) % 4) * 2 + zl
    b_m = ((y + 3) % 4) * 2 + zl
    b_f = ((y + 2) % 4) * 2 + zl
    b_z = y * 2 + 1 - zl
    b_pz = ((y + 1) % 4) * 2 + 1 - zl
    b_mz = ((y + 3) % 4) * 2 + 1 - zl
    b_fz = ((y + 2) % 4) * 2 + 1 - zl
    pw_out = (b_fz, b_f, b_pz, b_mz, b_p, b_m, b_z)
    pw_in = (b_fz, b_f, b_mz, b_pz, b_m, b_p, b_z)
    pending = []

    pair_c = x * 8 + zh * 2 + 1 - core

    def send(src, dst, s_sem, r_sem, pair=None, pw=None):
        copy = pltpu.make_async_remote_copy(
            src_ref=src, dst_ref=dst, send_sem=s_sem, recv_sem=r_sem,
            device_id={"pair": a if pair is None else pair, "pw": b if pw is None else pw},
            device_id_type=MESH,
        )
        copy.start()
        return copy

    def arrived(slot, sem):
        pltpu.make_async_copy(slot, slot, sem).wait()

    barrier = pltpu.get_barrier_semaphore()
    z_other = (zh + 3 + 2 * zl) % 4
    peers = [(a, b_p), (a, b_m), (a, b_z), (x * 8 + z_other * 2 + core, b_z), (pair_c, b)]
    peers += [(((x + j) % 4) * 8 + zh * 2 + core, b) for j in (1, 3)]

    def greet(sem):
        for pair, pw in peers:
            pl.semaphore_signal(sem, inc=1, device_id={"pair": pair, "pw": pw}, device_id_type=MESH)

    greet(barrier)
    x_load = pltpu.make_async_copy(x_hbm, xv, sem_local.at[0])
    t_load = pltpu.make_async_copy(t_hbm, tv, sem_local.at[1])
    d_loads = [
        pltpu.make_async_copy(d_hbm.at[0, pl.ds(h * 256, 256)], dv.at[2 * b + h], sem_local.at[2 + h]) for h in range(2)
    ]
    w_loads = [
        pltpu.make_async_copy(w_hbm.at[0, pl.ds(i * 128, 128)], wv.at[pl.ds(i * 128, 128)], sem_local.at[4 + i])
        for i in range(4)
    ]
    for load in d_loads:
        load.start()
    x_load.start()
    small_loads = [
        pltpu.make_async_copy(src, dst, sem_local.at[8 + i])
        for i, (src, dst) in enumerate((
            (index_hbm, index_ref), (weight_hbm, weight_ref), (bands_hbm, bands_ref), (energy_hbm, energy_ref)
        ))
    ]
    for load in [*small_loads, t_load, *w_loads]:
        load.start()
    for load in d_loads:
        load.wait()
    pl.semaphore_wait(barrier, len(peers))
    greet(rounds.at[0])

    M0, M1A, M1B, F0, MZ0, MZ1, P1, P0A, P0B, F1, PZ0, PZ1, Z0, Z1, FZ0, FZ1 = range(16)
    sent = [0]

    def relay(src, dst, role, pw):
        pending.append(send(src, dst, sa_s.at[sent[0]], sa_r.at[role], pw=pw))
        sent[0] += 1

    def quarter(h, r):
        return dv.at[2 * b + h, pl.ds(r * 128, 128)]

    own = [dv.at[2 * b + h] for h in range(2)]
    quarters = [[quarter(h, r) for r in range(2)] for h in range(2)]
    relay(own[0], dv.at[2 * b], M0, b_p)
    relay(own[1], dv.at[2 * b + 1], P1, b_m)
    relay(own[0], dv.at[2 * b], Z0, b_z)
    relay(quarters[1][0], quarter(1, 0), M1A, b_p)
    relay(quarters[0][0], quarter(0, 0), P0A, b_m)
    relay(own[1], dv.at[2 * b + 1], Z1, b_z)

    for load in small_loads:
        load.wait()

    tab[...] = jnp.zeros_like(tab)
    tab[:, 0:4, 0:16] = index_ref[...].astype(F32)
    tab[:, 4:8, 0:16] = weight_ref[...].astype(F32)
    tb[b] = tab[...].reshape(32, 128).astype(BF)
    own_bands = jnp.where(iota((16, 128), 1) == 16 * b + iota((16, 128), 0), bands_ref[...].astype(F32), 0.0)
    own_bands = jnp.sum(own_bands, axis=1, keepdims=True)
    live = ((iota((16, 256), 1) % NCOND).astype(F32) < own_bands).astype(F32)
    live = jnp.concatenate([live] * 4, axis=0)
    energy = jnp.concatenate([energy_ref[pl.ds(u, 16, stride=2), :] for u in range(2)], axis=1)
    energy = jnp.concatenate([energy] * 4, axis=0)
    chosen = (iota((8, 128), 1) == 4 * a + iota((8, 128), 0)) & (iota((8, 128), 0) < 4)
    chosen = chosen.astype(F32).astype(BF)
    x_load.wait()
    for k in range(16):
        picked = dot_t(chosen, xv[k * 256 : (k + 1) * 256, :])
        for n in range(4):
            rows_x[n * 16 + k : n * 16 + k + 1, :] = picked[n : n + 1, :]
    for i in range(2):
        pl.semaphore_wait(rounds.at[i], len(peers))
        greet(rounds.at[i + 1])
    for j, dest in enumerate(pw_out):
        pending.append(send(tb.at[b], tb.at[b], sq_s.at[j], sq_r.at[j], pw=dest))

    z_of = (zh, (zh + 1) % 4, (zh + 3) % 4, (zh + 2) % 4)
    x_of = (x, (x + 1) % 4, (x + 3) % 4, (x + 2) % 4)
    from_of = (0, 2, 1, 3)

    def gather(buf, n):
        def move(part, index, pair):
            pending.append(send(part, part, sg_s.at[n, index], sg_r.at[n, index], pair=pair))

        def x_out(p):
            for i in (3, 1, 2):
                move(buf.at[x, z_of[p], core], 3 * p + i + 2, x_of[i] * 8 + zh * 2 + core)

        def x_in(p):
            for i in (1, 2, 3):
                arrived(buf.at[x_of[i], z_of[p], core], sg_r.at[n, 3 * p + from_of[i] + 2])
            move(buf.at[:, z_of[p], core], 15 + p, pair_c)

        def z_in(i):
            arrived(buf.at[x, z_of[i], core], sg_r.at[n, from_of[i] - 1])
            x_out(i)

        for i in (3, 1, 2):
            move(buf.at[x, zh, core], i - 1, x * 8 + z_of[i] * 2 + core)
        x_out(0)
        yield
        z_in(1)
        z_in(2)
        yield
        z_in(3)
        x_in(0)
        yield
        x_in(1)
        x_in(2)
        yield
        x_in(3)
        yield
        for p in range(4):
            arrived(buf.at[:, z_of[p], 1 - core], sg_r.at[n, 15 + p])
        yield

    row_k = iota((64, 256), 0) % 16
    lane = iota((16, 128), 1)

    def transforms(rows, transposed):
        def step(k, total):
            mine = jnp.where(row_k == k, rows, 0.0).astype(BF)
            return total + (dot_t if transposed else dot)(mine, tv[k])

        return lax.fori_loop(0, 16, step, jnp.zeros((64, 256), F32), unroll=16)

    def spread_columns(app, rows):
        for part in range(8):
            i, half = part % 4, part // 4
            block = jnp.zeros((16, 128), F32)
            for n in range(4):
                piece = rows[n * 16 : n * 16 + 16, half * 128 : half * 128 + 128]
                shift = ((n - i) * 32) % 128
                if shift:
                    piece = pltpu.roll(piece, shift, axis=1)
                block = jnp.where(lane // 32 == n, piece, block)
            ysend[app, part] = block.astype(BF)
        yrecv[app, b] = ysend[app, b]
        for j, dest in enumerate(pw_out):
            pending.append(send(ysend.at[app, dest], yrecv.at[app, b], sy_s.at[app, j], sy_r.at[app, j], pw=dest))

    t_load.wait()
    spread_columns(0, transforms(live * rows_x[...], True))

    def accumulate(slot, first=False):
        columns = pl.ds(pl.multiple_of(slot * 256, 256), 256)
        product = dot(wv[:, columns], dv[slot])
        if first:
            acc[...] = product
        else:
            acc[...] += product

    arrived(dv.at[2 * b_m], sa_r.at[M0])
    relay(dv.at[2 * b_m], dv.at[2 * b_m], F0, b_p)
    relay(quarters[1][1], quarter(1, 1), M1B, b_p)
    arrived(dv.at[2 * b_p + 1], sa_r.at[P1])
    relay(dv.at[2 * b_p + 1], dv.at[2 * b_p + 1], F1, b_m)
    relay(quarters[0][1], quarter(0, 1), P0B, b_m)

    table_lane = iota((32, 128), 1) // 16
    table_rows = jnp.zeros((32, 128), F32)
    for j, source in enumerate(pw_in):
        arrived(tb.at[source], sq_r.at[j])
    for s in range(8):
        piece = tb[s].astype(F32)
        if s:
            piece = pltpu.roll(piece, 16 * s, axis=1)
        table_rows = jnp.where(table_lane == s, piece, table_rows)
    t2[x, zh, core] = table_rows.astype(BF)
    pl.semaphore_wait(rounds.at[2], len(peers))
    table_gather = gather(t2, 0)
    next(table_gather)

    for h, role in ((0, Z0), (1, Z1)):
        slot = 2 * b_z + h
        arrived(dv.at[slot], sa_r.at[role])
        relay(dv.at[slot], dv.at[slot], (MZ0, MZ1)[h], b_p)
        relay(dv.at[slot], dv.at[slot], (PZ0, PZ1)[h], b_m)
    for load in w_loads:
        load.wait()
    accumulate(2 * b, True)
    accumulate(2 * b + 1)
    for h, role in ((0, F0), (1, F1)):
        slot = 2 * b_f + h
        arrived(dv.at[slot], sa_r.at[role])
        relay(dv.at[slot], dv.at[slot], (FZ0, FZ1)[h], b_z)
    for slot in (2 * b_m, 2 * b_p + 1, 2 * b_z, 2 * b_z + 1, 2 * b_f, 2 * b_f + 1):
        accumulate(slot)
    next(table_gather)
    for slot, roles in ((2 * b_m + 1, (M1A, M1B)), (2 * b_p, (P0A, P0B))):
        for r in range(2):
            arrived(dv.at[slot, pl.ds(r * 128, 128)], sa_r.at[roles[r]])
        accumulate(slot)
    for slot, role in ((2 * b_mz, MZ0), (2 * b_pz, PZ0)):
        arrived(dv.at[slot], sa_r.at[role])
        accumulate(slot)
    next(table_gather)
    for slot, role in ((2 * b_fz, FZ0), (2 * b_mz + 1, MZ1), (2 * b_pz + 1, PZ1), (2 * b_fz + 1, FZ1)):
        arrived(dv.at[slot], sa_r.at[role])
        accumulate(slot)

    applied = acc[...].astype(BF)
    raw = jnp.zeros((256, 256), F32)
    for h in range(2):
        raw += lax.dot_general(
            dv[2 * b + h], applied[h * 256 : h * 256 + 256], (((0,), (0,)), ((), ())), preferred_element_type=F32
        )
    kp[...] = (0.5 * (raw + raw.T)).astype(BF).reshape(8, 32, 256)
    for j, dest in enumerate(pw_out):
        pending.append(send(kp.at[dest], kr.at[b], sk_s.at[j], sk_r.at[j], pw=dest))
    kr[b] = kp[b]

    for _ in table_gather:
        pass
    t2f[...] = t2[...].reshape(1024, 128).astype(F32)

    def coefficients(i, carry):
        for h in range(2):
            this = (2 * i + h).astype(F32)
            total = jnp.zeros((128, 128), F32)
            for j in range(4):
                index = t2f[pl.ds(j, 128, stride=8), :]
                weight = t2f[pl.ds(4 + j, 128, stride=8), :]
                total += jnp.where(index == this, weight, 0.0)
            ct[i, :, h * 128 : h * 128 + 128] = total.astype(BF)
        return carry

    lax.fori_loop(0, 16, coefficients, 0)

    for j, source in enumerate(pw_in):
        arrived(kr.at[source], sk_r.at[j])
    total = kr[0].astype(F32)
    for j in range(1, 8):
        total += kr[j].astype(F32)
    kt[x, zh, core] = total.astype(BF)
    kernel_gather = gather(kt, 1)
    next(kernel_gather)

    def mix(app):
        for j, source in enumerate(pw_in):
            arrived(yrecv.at[app, source], sy_r.at[app, j])
        columns = yrecv[app].reshape(128, 128).astype(F32).T.astype(BF)

        def step(i, carry):
            mixed = dot(columns, ct[i]).astype(BF)
            for h in range(2):
                for n in range(4):
                    ucat[2 * i + h, :, n * 128 : n * 128 + 128] = mixed[
                        n * 32 : n * 32 + 32, h * 128 : h * 128 + 128
                    ]
            return carry

        lax.fori_loop(0, 16, step, 0, unroll=8)

    def contract(app):
        product = dot(kcat[...], ucat[...].reshape(1024, 512))
        zs[app] = product.T.astype(BF).reshape(4, 128, 256)
        part = pl.ds(pl.multiple_of(b * 16, 16), 16)
        zr[app, b] = zs[app, :, part, :]
        for j, dest in enumerate(pw_out):
            part = pl.ds(pl.multiple_of(dest * 16, 16), 16)
            pending.append(send(zs.at[app, :, part, :], zr.at[app, b], sz_s.at[app, j], sz_r.at[app, j], pw=dest))

    def summed(app):
        for j, source in enumerate(pw_in):
            arrived(zr.at[app, source], sz_r.at[app, j])
        rows = zr[app, 0].astype(F32)
        for j in range(1, 8):
            rows += zr[app, j].astype(F32)
        return rows.reshape(64, 256)

    norm_scale = 1.0 / math.sqrt(32768.0)
    def finish(app, vector):
        return norm_scale * live * transforms(summed(app), False) + energy * vector

    mix(0)
    for _ in kernel_gather:
        pass
    for i in range(8):
        rows = kt[i // 2, 2 * (i % 2) : 2 * (i % 2) + 2].reshape(128, 256)
        kcat[:, i * 128 : i * 128 + 128] = rows.astype(F32).T.astype(BF)
    contract(0)
    first = finish(0, rows_x[...]).astype(BF)
    first_wide = first.astype(F32)
    spread_columns(1, transforms(live * first_wide, True))

    r_in, r_out = iota((64, 64), 1), iota((64, 64), 0)
    order = (r_in == ((r_out // 4) % 4) * 16 + (r_out // 16) * 4 + r_out % 4).astype(F32).astype(BF)
    fs[...] = dot(order, first).astype(BF).reshape(4, 16, 256)
    first_sends = []
    for i in range(4):
        target = 4 * b + i

        @pl.when(target == a)
        def _():
            fb[a] = fs[i]

        @pl.when(target != a)
        def _():
            send(fs.at[i], fb.at[a], sf_s.at[i], sf_r.at[a], pair=target)

    mix(1)
    contract(1)

    root = a // 4
    d_y = (y + 4 - root // 2) % 4
    d_z = (zl + root % 2) % 2
    is_root = (d_y == 0) & (d_z == 0)

    @pl.when(b == root)
    def _():
        def take(s, carry):
            @pl.when(s != a)
            def _():
                arrived(fb.at[s], sf_r.at[s])

            return carry

        lax.fori_loop(0, 32, take, 0)
        wide = fb[...].reshape(512, 256).astype(F32)
        for u in range(2):
            fbf[u] = wide[:, u * 128 : u * 128 + 128]
        for k in range(4):
            for u in range(2):
                at = k * 256 + u * 128
                out1[at : at + 128, :] = fbf[u, pl.ds(k, 128, stride=4), :].T.astype(BF)

    def half(h):
        return out1.at[pl.ds(h * 512, 512)]

    def pass_on(h, pw, slot):
        return pltpu.make_async_remote_copy(
            src_ref=half(h), dst_ref=half(h), send_sem=sb_s.at[slot], recv_sem=sb_r.at[h],
            device_id={"pair": a, "pw": pw}, device_id_type=MESH,
        )

    to_p = [pass_on(h, b_p, h) for h in range(2)]
    to_m = [pass_on(h, b_m, 2 + h) for h in range(2)]
    to_z = [pass_on(h, b_z, 4 + h) for h in range(2)]

    @pl.when(is_root)
    def _():
        to_z[0].start()
        for h in range(2):
            to_p[h].start()
            to_m[1 - h].start()

    second = 2.0 * finish(1, first_wide) - rows_x[...]
    g[x, zh, core] = second.astype(BF)
    last_gather = gather(g, 2)
    next(last_gather)

    @pl.when(is_root)
    def _():
        to_z[1].start()

    next(last_gather)
    for d, h, to_far in ((1, 0, to_p), (3, 1, to_m)):

        @pl.when((d_y == d) & (d_z == 0))
        def _():
            arrived(half(h), sb_r.at[h])
            to_far[h].start()
            to_z[h].start()

    next(last_gather)
    for d, h in ((1, 0), (3, 1)):

        @pl.when((d_y == d) & (d_z == 0))
        def _():
            arrived(half(1 - h), sb_r.at[1 - h])
            to_z[1 - h].start()

    next(last_gather)
    for d, h, to_far in ((1, 0, to_p), (3, 1, to_m)):

        @pl.when((d_y == d) & (d_z == 1))
        def _():
            arrived(half(h), sb_r.at[h])
            to_far[h].start()

    next(last_gather)
    next(last_gather)
    for d, h in ((1, 0), (3, 1)):

        @pl.when((d_y == d) & (d_z == 1))
        def _():
            arrived(half(1 - h), sb_r.at[1 - h])

    @pl.when((d_y == 2) | ((d_y == 0) & (d_z == 1)))
    def _():
        for h in range(2):
            arrived(half(h), sb_r.at[h])

    for copy in pending:
        copy.wait_send()
    for i in range(4):
        target = 4 * b + i

        @pl.when(target != a)
        def _():
            pltpu.make_async_copy(fs.at[i], fs.at[i], sf_s.at[i]).wait()

    @pl.when(is_root)
    def _():
        for h in range(2):
            to_p[h].wait_send()
            to_m[h].wait_send()

    @pl.when((d_z == 0) & (d_y != 2))
    def _():
        for h in range(2):
            to_z[h].wait_send()

    @pl.when(d_y == 1)
    def _():
        to_p[0].wait_send()

    @pl.when(d_y == 3)
    def _():
        to_m[1].wait_send()


def layout(first_ref, g_ref, out1, out2, wide, stage, sem):
    copies = [pltpu.make_async_copy(first_ref, out1, sem.at[4])]
    copies[0].start()
    rows = g_ref[...].reshape(2048, 256).astype(F32)
    for u in range(2):
        wide[u] = rows[:, u * 128 : u * 128 + 128]
    for i in range(4):
        for k in range(4 * i, 4 * i + 4):
            for u in range(2):
                at = k * 256 + u * 128
                stage[at : at + 128, :] = wide[u, pl.ds(k, 128, stride=16), :].T
        part = pl.ds(i * 1024, 1024)
        copies.append(pltpu.make_async_copy(stage.at[part], out2.at[part], sem.at[i]))
        copies[-1].start()
    for copy in copies:
        copy.wait()


def shards(screened, density, transform, energy, trial, coarse_index, interp_weight, bands):
    hbm = pl.BlockSpec(memory_space=pltpu.HBM)
    vmem = pl.BlockSpec(memory_space=pltpu.VMEM)
    dma = pltpu.SemaphoreType.DMA
    first, gathered = pl.pallas_call(
        kernel,
        out_shape=(jax.ShapeDtypeStruct((1024, 128), BF), jax.ShapeDtypeStruct((4, 4, 2, 64, 256), BF)),
        in_specs=[hbm] * 8,
        out_specs=(vmem, vmem),
        scratch_shapes=[
            pltpu.VMEM((512, 4096), BF),
            pltpu.VMEM((16, 256, 256), BF),
            pltpu.VMEM((16, 256, 256), BF),
            pltpu.VMEM((4096, 128), BF),
            pltpu.VMEM((512, 256), F32),
            pltpu.VMEM((8, 32, 256), BF),
            pltpu.VMEM((8, 32, 256), BF),
            pltpu.VMEM((4, 4, 2, 32, 256), BF),
            pltpu.VMEM((256, 1024), BF),
            pltpu.VMEM((4, 8, 128), F32),
            pltpu.VMEM((8, 32, 128), BF),
            pltpu.VMEM((4, 4, 2, 32, 128), BF),
            pltpu.VMEM((1024, 128), F32),
            pltpu.VMEM((16, 128, 256), BF),
            pltpu.VMEM((32, 32, 512), BF),
            pltpu.VMEM((2, 8, 16, 128), BF),
            pltpu.VMEM((2, 8, 16, 128), BF),
            pltpu.VMEM((2, 4, 128, 256), BF),
            pltpu.VMEM((2, 8, 4, 16, 256), BF),
            pltpu.VMEM((64, 256), F32),
            pltpu.VMEM((4, 16, 256), BF),
            pltpu.VMEM((32, 16, 256), BF),
            pltpu.VMEM((2, 512, 128), F32),
            pltpu.VMEM((1, 128), jnp.int32),
            pltpu.VMEM((32, 128), F32),
            pltpu.VMEM((4, 4, 16), jnp.int32),
            pltpu.VMEM((4, 4, 16), BF),
            pltpu.SemaphoreType.REGULAR((3,)),
            dma((12,)),
            dma((16,)), dma((16,)),
            dma((6,)), dma((2,)),
            dma((2, 7)), dma((2, 7)),
            dma((7,)), dma((7,)),
            dma((2, 7)), dma((2, 7)),
            dma((7,)), dma((7,)),
            dma((3, 19)), dma((3, 19)),
            dma((4,)), dma((32,)),
        ],
        compiler_params=pltpu.CompilerParams(
            collective_id=0, has_side_effects=True, vmem_limit_bytes=48 * 1024 * 1024
        ),
        name="bse_chebyshev",
    )(
        *[
            pltpu.with_memory_space_constraint(value, pltpu.HBM)
            for value in (
                screened, density, transform, trial, bands.reshape(1, 128), energy.reshape(32, 128),
                jnp.transpose(coarse_index, (0, 2, 1)), jnp.transpose(interp_weight, (0, 2, 1)),
            )
        ]
    )
    return pl.pallas_call(
        layout,
        out_shape=(jax.ShapeDtypeStruct((1024, 128), BF), jax.ShapeDtypeStruct((4096, 128), F32)),
        in_specs=[vmem] * 2,
        out_specs=(hbm, hbm),
        scratch_shapes=[pltpu.VMEM((2, 2048, 128), F32), pltpu.VMEM((4096, 128), F32), dma((5,))],
        compiler_params=pltpu.CompilerParams(vmem_limit_bytes=48 * 1024 * 1024),
        name="layout",
    )(first, gathered)


def solution(mesh):
    in_specs = (
        P("pair", "pw", None),
        P("pair", "pw", None),
        P("pw", None, None),
        P("pw"),
        P("pw", None),
        P("pair", "pw", None),
        P("pair", "pw", None),
        P(),
    )
    out_specs = (P("pair", None), P("pw", None))
    return jax.shard_map(shards, mesh=mesh, in_specs=in_specs, out_specs=out_specs, check_vma=False)
```

```python
import math

import jax
import jax.numpy as jnp
from jax import lax
from jax.experimental import pallas as pl
from jax.experimental.pallas import tpu as pltpu
from jax.sharding import PartitionSpec as P

MESH = pl.DeviceIdType.MESH
BF = jnp.bfloat16
F32 = jnp.float32
NCOND = 16


def dot(lhs, rhs):
    return jnp.dot(lhs, rhs, preferred_element_type=F32)


def dot_t(lhs, rhs):
    return lax.dot_general(lhs, rhs, (((1,), (1,)), ((), ())), preferred_element_type=F32)


def iota(shape, dim):
    return lax.broadcasted_iota(jnp.int32, shape, dim)


def kernel(
    w_hbm, d_hbm, t_hbm, x_hbm, bands_hbm, energy_hbm, index_hbm, weight_hbm,
    out1, g,
    wv, dv, tv, xv, acc, kp, kr, kt, kcat, tab, tb, t2, t2f, ct, ucat, ysend, yrecv, zs, zr,
    rows_x, fs, fb, fbf, bands_ref, energy_ref, index_ref, weight_ref,
    rounds, sem_local, sa_s, sa_r, sb_s, sb_r, sy_s, sy_r, sk_s, sk_r, sz_s, sz_r, sq_s, sq_r,
    sg_s, sg_r, sf_s, sf_r,
):
    a = lax.axis_index("pair")
    b = lax.axis_index("pw")
    x, zh, core = a // 8, (a // 2) % 4, a % 2
    y, zl = b // 2, b % 2
    b_p = ((y + 1) % 4) * 2 + zl
    b_m = ((y + 3) % 4) * 2 + zl
    b_f = ((y + 2) % 4) * 2 + zl
    b_z = y * 2 + 1 - zl
    b_pz = ((y + 1) % 4) * 2 + 1 - zl
    b_mz = ((y + 3) % 4) * 2 + 1 - zl
    b_fz = ((y + 2) % 4) * 2 + 1 - zl
    pw_out = (b_fz, b_f, b_pz, b_mz, b_p, b_m, b_z)
    pw_in = (b_fz, b_f, b_mz, b_pz, b_m, b_p, b_z)
    pending = []

    pair_c = x * 8 + zh * 2 + 1 - core

    def send(src, dst, s_sem, r_sem, pair=None, pw=None):
        copy = pltpu.make_async_remote_copy(
            src_ref=src, dst_ref=dst, send_sem=s_sem, recv_sem=r_sem,
            device_id={"pair": a if pair is None else pair, "pw": b if pw is None else pw},
            device_id_type=MESH,
        )
        copy.start()
        return copy

    def arrived(slot, sem):
        pltpu.make_async_copy(slot, slot, sem).wait()

    barrier = pltpu.get_barrier_semaphore()
    z_other = (zh + 3 + 2 * zl) % 4
    peers = [(a, b_p), (a, b_m), (a, b_z), (x * 8 + z_other * 2 + core, b_z), (pair_c, b)]
    peers += [(((x + j) % 4) * 8 + zh * 2 + core, b) for j in (1, 3)]

    def greet(sem):
        for pair, pw in peers:
            pl.semaphore_signal(sem, inc=1, device_id={"pair": pair, "pw": pw}, device_id_type=MESH)

    greet(barrier)
    x_load = pltpu.make_async_copy(x_hbm, xv, sem_local.at[0])
    t_load = pltpu.make_async_copy(t_hbm, tv, sem_local.at[1])
    d_loads = [
        pltpu.make_async_copy(d_hbm.at[0, pl.ds(h * 256, 256)], dv.at[2 * b + h], sem_local.at[2 + h]) for h in range(2)
    ]
    w_loads = [
        pltpu.make_async_copy(w_hbm.at[0, pl.ds(i * 128, 128)], wv.at[pl.ds(i * 128, 128)], sem_local.at[4 + i])
        for i in range(4)
    ]
    for load in d_loads:
        load.start()
    x_load.start()
    small_loads = [
        pltpu.make_async_copy(src, dst, sem_local.at[8 + i])
        for i, (src, dst) in enumerate((
            (index_hbm, index_ref), (weight_hbm, weight_ref), (bands_hbm, bands_ref), (energy_hbm, energy_ref)
        ))
    ]
    for load in [*small_loads, t_load, *w_loads]:
        load.start()
    for load in d_loads:
        load.wait()
    pl.semaphore_wait(barrier, len(peers))
    greet(rounds.at[0])

    M0, M1A, M1B, F0, MZ0, MZ1, P1, P0A, P0B, F1, PZ0, PZ1, Z0, Z1, FZ0, FZ1 = range(16)
    sent = [0]

    def relay(src, dst, role, pw):
        pending.append(send(src, dst, sa_s.at[sent[0]], sa_r.at[role], pw=pw))
        sent[0] += 1

    def quarter(h, r):
        return dv.at[2 * b + h, pl.ds(r * 128, 128)]

    own = [dv.at[2 * b + h] for h in range(2)]
    quarters = [[quarter(h, r) for r in range(2)] for h in range(2)]
    relay(own[0], dv.at[2 * b], M0, b_p)
    relay(own[1], dv.at[2 * b + 1], P1, b_m)
    relay(own[0], dv.at[2 * b], Z0, b_z)
    relay(quarters[1][0], quarter(1, 0), M1A, b_p)
    relay(quarters[0][0], quarter(0, 0), P0A, b_m)
    relay(own[1], dv.at[2 * b + 1], Z1, b_z)

    for load in small_loads:
        load.wait()

    tab[...] = jnp.zeros_like(tab)
    tab[:, 0:4, 0:16] = index_ref[...].astype(F32)
    tab[:, 4:8, 0:16] = weight_ref[...].astype(F32)
    tb[b] = tab[...].reshape(32, 128).astype(BF)
    own_bands = jnp.where(iota((16, 128), 1) == 16 * b + iota((16, 128), 0), bands_ref[...].astype(F32), 0.0)
    own_bands = jnp.sum(own_bands, axis=1, keepdims=True)
    live = ((iota((16, 256), 1) % NCOND).astype(F32) < own_bands).astype(F32)
    live = jnp.concatenate([live] * 4, axis=0)
    energy = jnp.concatenate([energy_ref[pl.ds(u, 16, stride=2), :] for u in range(2)], axis=1)
    energy = jnp.concatenate([energy] * 4, axis=0)
    chosen = (iota((8, 128), 1) == 4 * a + iota((8, 128), 0)) & (iota((8, 128), 0) < 4)
    chosen = chosen.astype(F32).astype(BF)
    x_load.wait()
    for k in range(16):
        picked = dot_t(chosen, xv[k * 256 : (k + 1) * 256, :])
        for n in range(4):
            rows_x[n * 16 + k : n * 16 + k + 1, :] = picked[n : n + 1, :]
    for i in range(2):
        pl.semaphore_wait(rounds.at[i], len(peers))
        greet(rounds.at[i + 1])
    for j, dest in enumerate(pw_out):
        pending.append(send(tb.at[b], tb.at[b], sq_s.at[j], sq_r.at[j], pw=dest))

    z_of = (zh, (zh + 1) % 4, (zh + 3) % 4, (zh + 2) % 4)
    x_of = (x, (x + 1) % 4, (x + 3) % 4, (x + 2) % 4)
    from_of = (0, 2, 1, 3)

    def gather(buf, n):
        def move(part, index, pair):
            pending.append(send(part, part, sg_s.at[n, index], sg_r.at[n, index], pair=pair))

        def x_out(p):
            for i in (3, 1, 2):
                move(buf.at[x, z_of[p], core], 3 * p + i + 2, x_of[i] * 8 + zh * 2 + core)

        def x_in(p):
            for i in (1, 2, 3):
                arrived(buf.at[x_of[i], z_of[p], core], sg_r.at[n, 3 * p + from_of[i] + 2])
            move(buf.at[:, z_of[p], core], 15 + p, pair_c)

        def z_in(i):
            arrived(buf.at[x, z_of[i], core], sg_r.at[n, from_of[i] - 1])
            x_out(i)

        for i in (3, 1, 2):
            move(buf.at[x, zh, core], i - 1, x * 8 + z_of[i] * 2 + core)
        x_out(0)
        yield
        z_in(1)
        z_in(2)
        yield
        z_in(3)
        x_in(0)
        yield
        x_in(1)
        x_in(2)
        yield
        x_in(3)
        yield
        for p in range(4):
            arrived(buf.at[:, z_of[p], 1 - core], sg_r.at[n, 15 + p])
        yield

    row_k = iota((64, 256), 0) % 16
    lane = iota((16, 128), 1)

    def transforms(rows, transposed):
        def step(k, total):
            mine = jnp.where(row_k == k, rows, 0.0).astype(BF)
            return total + (dot_t if transposed else dot)(mine, tv[k])

        return lax.fori_loop(0, 16, step, jnp.zeros((64, 256), F32), unroll=16)

    def spread_columns(app, rows):
        for part in range(8):
            i, half = part % 4, part // 4
            block = jnp.zeros((16, 128), F32)
            for n in range(4):
                piece = rows[n * 16 : n * 16 + 16, half * 128 : half * 128 + 128]
                shift = ((n - i) * 32) % 128
                if shift:
                    piece = pltpu.roll(piece, shift, axis=1)
                block = jnp.where(lane // 32 == n, piece, block)
            ysend[app, part] = block.astype(BF)
        yrecv[app, b] = ysend[app, b]
        for j, dest in enumerate(pw_out):
            pending.append(send(ysend.at[app, dest], yrecv.at[app, b], sy_s.at[app, j], sy_r.at[app, j], pw=dest))

    t_load.wait()
    spread_columns(0, transforms(live * rows_x[...], True))

    def accumulate(slot, first=False):
        columns = pl.ds(pl.multiple_of(slot * 256, 256), 256)
        product = dot(wv[:, columns], dv[slot])
        if first:
            acc[...] = product
        else:
            acc[...] += product

    arrived(dv.at[2 * b_m], sa_r.at[M0])
    relay(dv.at[2 * b_m], dv.at[2 * b_m], F0, b_p)
    relay(quarters[1][1], quarter(1, 1), M1B, b_p)
    arrived(dv.at[2 * b_p + 1], sa_r.at[P1])
    relay(dv.at[2 * b_p + 1], dv.at[2 * b_p + 1], F1, b_m)
    relay(quarters[0][1], quarter(0, 1), P0B, b_m)

    table_lane = iota((32, 128), 1) // 16
    table_rows = jnp.zeros((32, 128), F32)
    for j, source in enumerate(pw_in):
        arrived(tb.at[source], sq_r.at[j])
    for s in range(8):
        piece = tb[s].astype(F32)
        if s:
            piece = pltpu.roll(piece, 16 * s, axis=1)
        table_rows = jnp.where(table_lane == s, piece, table_rows)
    t2[x, zh, core] = table_rows.astype(BF)
    pl.semaphore_wait(rounds.at[2], len(peers))
    table_gather = gather(t2, 0)
    next(table_gather)

    for h, role in ((0, Z0), (1, Z1)):
        slot = 2 * b_z + h
        arrived(dv.at[slot], sa_r.at[role])
        relay(dv.at[slot], dv.at[slot], (MZ0, MZ1)[h], b_p)
        relay(dv.at[slot], dv.at[slot], (PZ0, PZ1)[h], b_m)
    for load in w_loads:
        load.wait()
    accumulate(2 * b, True)
    accumulate(2 * b + 1)
    for h, role in ((0, F0), (1, F1)):
        slot = 2 * b_f + h
        arrived(dv.at[slot], sa_r.at[role])
        relay(dv.at[slot], dv.at[slot], (FZ0, FZ1)[h], b_z)
    for slot in (2 * b_m, 2 * b_p + 1, 2 * b_z, 2 * b_z + 1, 2 * b_f, 2 * b_f + 1):
        accumulate(slot)
    next(table_gather)
    for slot, roles in ((2 * b_m + 1, (M1A, M1B)), (2 * b_p, (P0A, P0B))):
        for r in range(2):
            arrived(dv.at[slot, pl.ds(r * 128, 128)], sa_r.at[roles[r]])
        accumulate(slot)
    for slot, role in ((2 * b_mz, MZ0), (2 * b_pz, PZ0)):
        arrived(dv.at[slot], sa_r.at[role])
        accumulate(slot)
    next(table_gather)
    for last in (((2 * b_fz, FZ0), (2 * b_mz + 1, MZ1)), ((2 * b_pz + 1, PZ1), (2 * b_fz + 1, FZ1))):
        for slot, role in last:
            arrived(dv.at[slot], sa_r.at[role])
            accumulate(slot)
        next(table_gather)

    applied = acc[...].astype(BF)
    raw = jnp.zeros((256, 256), F32)
    for h in range(2):
        raw += lax.dot_general(
            dv[2 * b + h], applied[h * 256 : h * 256 + 256], (((0,), (0,)), ((), ())), preferred_element_type=F32
        )
    kp[...] = (0.5 * (raw + raw.T)).astype(BF).reshape(8, 32, 256)
    for j, dest in enumerate(pw_out):
        pending.append(send(kp.at[dest], kr.at[b], sk_s.at[j], sk_r.at[j], pw=dest))
    kr[b] = kp[b]

    for _ in table_gather:
        pass
    t2f[...] = t2[...].reshape(1024, 128).astype(F32)

    def coefficients(i, carry):
        totals = [jnp.zeros((128, 128), F32)] * 2
        for j in range(4):
            index = t2f[pl.ds(j, 128, stride=8), :]
            weight = t2f[pl.ds(4 + j, 128, stride=8), :]
            for h in range(2):
                totals[h] += jnp.where(index == (2 * i + h).astype(F32), weight, 0.0)
        for h in range(2):
            ct[i, :, h * 128 : h * 128 + 128] = totals[h].astype(BF)
        return carry

    lax.fori_loop(0, 16, coefficients, 0)

    for j, source in enumerate(pw_in):
        arrived(kr.at[source], sk_r.at[j])
    total = kr[0].astype(F32)
    for j in range(1, 8):
        total += kr[j].astype(F32)
    kt[x, zh, core] = total.astype(BF)
    kernel_gather = gather(kt, 1)
    next(kernel_gather)

    def mix(app):
        for j, source in enumerate(pw_in):
            arrived(yrecv.at[app, source], sy_r.at[app, j])
        columns = yrecv[app].reshape(128, 128).astype(F32).T.astype(BF)

        def step(i, carry):
            mixed = dot(columns, ct[i]).astype(BF)
            for h in range(2):
                for n in range(4):
                    ucat[2 * i + h, :, n * 128 : n * 128 + 128] = mixed[
                        n * 32 : n * 32 + 32, h * 128 : h * 128 + 128
                    ]
            return carry

        lax.fori_loop(0, 16, step, 0, unroll=8)

    def contract(app):
        product = dot(kcat[...], ucat[...].reshape(1024, 512))
        zs[app] = product.T.astype(BF).reshape(4, 128, 256)
        part = pl.ds(pl.multiple_of(b * 16, 16), 16)
        zr[app, b] = zs[app, :, part, :]
        for j, dest in enumerate(pw_out):
            part = pl.ds(pl.multiple_of(dest * 16, 16), 16)
            pending.append(send(zs.at[app, :, part, :], zr.at[app, b], sz_s.at[app, j], sz_r.at[app, j], pw=dest))

    def summed(app):
        for j, source in enumerate(pw_in):
            arrived(zr.at[app, source], sz_r.at[app, j])
        rows = zr[app, 0].astype(F32)
        for j in range(1, 8):
            rows += zr[app, j].astype(F32)
        return rows.reshape(64, 256)

    norm_scale = 1.0 / math.sqrt(32768.0)
    def finish(app, vector):
        return norm_scale * live * transforms(summed(app), False) + energy * vector

    mix(0)
    for _ in kernel_gather:
        pass
    for i in range(8):
        rows = kt[i // 2, 2 * (i % 2) : 2 * (i % 2) + 2].reshape(128, 256)
        kcat[:, i * 128 : i * 128 + 128] = rows.astype(F32).T.astype(BF)
    contract(0)
    first = finish(0, rows_x[...]).astype(BF)
    first_wide = first.astype(F32)
    spread_columns(1, transforms(live * first_wide, True))

    r_in, r_out = iota((64, 64), 1), iota((64, 64), 0)
    order = (r_in == ((r_out // 4) % 4) * 16 + (r_out // 16) * 4 + r_out % 4).astype(F32).astype(BF)
    fs[...] = dot(order, first).astype(BF).reshape(4, 16, 256)
    first_sends = []
    for i in range(4):
        target = 4 * b + i

        @pl.when(target == a)
        def _():
            fb[a] = fs[i]

        @pl.when(target != a)
        def _():
            send(fs.at[i], fb.at[a], sf_s.at[i], sf_r.at[a], pair=target)

    mix(1)
    contract(1)

    root = a // 4
    d_y = (y + 4 - root // 2) % 4
    d_z = (zl + root % 2) % 2
    is_root = (d_y == 0) & (d_z == 0)

    @pl.when(b == root)
    def _():
        def take(s, carry):
            @pl.when(s != a)
            def _():
                arrived(fb.at[s], sf_r.at[s])

            return carry

        lax.fori_loop(0, 32, take, 0)
        wide = fb[...].reshape(512, 256).astype(F32)
        for u in range(2):
            fbf[u] = wide[:, u * 128 : u * 128 + 128]
        for k in range(4):
            for u in range(2):
                at = k * 256 + u * 128
                out1[at : at + 128, :] = fbf[u, pl.ds(k, 128, stride=4), :].T.astype(BF)

    def half(h):
        return out1.at[pl.ds(h * 512, 512)]

    def pass_on(h, pw, slot):
        return pltpu.make_async_remote_copy(
            src_ref=half(h), dst_ref=half(h), send_sem=sb_s.at[slot], recv_sem=sb_r.at[h],
            device_id={"pair": a, "pw": pw}, device_id_type=MESH,
        )

    to_p = [pass_on(h, b_p, h) for h in range(2)]
    to_m = [pass_on(h, b_m, 2 + h) for h in range(2)]
    to_z = [pass_on(h, b_z, 4 + h) for h in range(2)]

    @pl.when(is_root)
    def _():
        to_z[0].start()
        for h in range(2):
            to_p[h].start()
            to_m[1 - h].start()

    second = 2.0 * finish(1, first_wide) - rows_x[...]
    g[x, zh, core] = second.astype(BF)
    last_gather = gather(g, 2)
    next(last_gather)

    @pl.when(is_root)
    def _():
        to_z[1].start()

    next(last_gather)
    for d, h, to_far in ((1, 0, to_p), (3, 1, to_m)):

        @pl.when((d_y == d) & (d_z == 0))
        def _():
            arrived(half(h), sb_r.at[h])
            to_far[h].start()
            to_z[h].start()

    next(last_gather)
    for d, h in ((1, 0), (3, 1)):

        @pl.when((d_y == d) & (d_z == 0))
        def _():
            arrived(half(1 - h), sb_r.at[1 - h])
            to_z[1 - h].start()

    next(last_gather)
    for d, h, to_far in ((1, 0, to_p), (3, 1, to_m)):

        @pl.when((d_y == d) & (d_z == 1))
        def _():
            arrived(half(h), sb_r.at[h])
            to_far[h].start()

    next(last_gather)
    next(last_gather)
    for d, h in ((1, 0), (3, 1)):

        @pl.when((d_y == d) & (d_z == 1))
        def _():
            arrived(half(1 - h), sb_r.at[1 - h])

    @pl.when((d_y == 2) | ((d_y == 0) & (d_z == 1)))
    def _():
        for h in range(2):
            arrived(half(h), sb_r.at[h])

    for copy in pending:
        copy.wait_send()
    for i in range(4):
        target = 4 * b + i

        @pl.when(target != a)
        def _():
            pltpu.make_async_copy(fs.at[i], fs.at[i], sf_s.at[i]).wait()

    @pl.when(is_root)
    def _():
        for h in range(2):
            to_p[h].wait_send()
            to_m[h].wait_send()

    @pl.when((d_z == 0) & (d_y != 2))
    def _():
        for h in range(2):
            to_z[h].wait_send()

    @pl.when(d_y == 1)
    def _():
        to_p[0].wait_send()

    @pl.when(d_y == 3)
    def _():
        to_m[1].wait_send()


def layout(first_ref, g_ref, out1, out2, wide, stage, sem):
    copies = [pltpu.make_async_copy(first_ref, out1, sem.at[4])]
    copies[0].start()
    rows = g_ref[...].reshape(2048, 256).astype(F32)
    for u in range(2):
        wide[u] = rows[:, u * 128 : u * 128 + 128]
    for i in range(4):
        for k in range(4 * i, 4 * i + 4):
            for u in range(2):
                at = k * 256 + u * 128
                stage[at : at + 128, :] = wide[u, pl.ds(k, 128, stride=16), :].T
        part = pl.ds(i * 1024, 1024)
        copies.append(pltpu.make_async_copy(stage.at[part], out2.at[part], sem.at[i]))
        copies[-1].start()
    for copy in copies:
        copy.wait()


def shards(screened, density, transform, energy, trial, coarse_index, interp_weight, bands):
    hbm = pl.BlockSpec(memory_space=pltpu.HBM)
    vmem = pl.BlockSpec(memory_space=pltpu.VMEM)
    dma = pltpu.SemaphoreType.DMA
    first, gathered = pl.pallas_call(
        kernel,
        out_shape=(jax.ShapeDtypeStruct((1024, 128), BF), jax.ShapeDtypeStruct((4, 4, 2, 64, 256), BF)),
        in_specs=[hbm] * 8,
        out_specs=(vmem, vmem),
        scratch_shapes=[
            pltpu.VMEM((512, 4096), BF),
            pltpu.VMEM((16, 256, 256), BF),
            pltpu.VMEM((16, 256, 256), BF),
            pltpu.VMEM((4096, 128), BF),
            pltpu.VMEM((512, 256), F32),
            pltpu.VMEM((8, 32, 256), BF),
            pltpu.VMEM((8, 32, 256), BF),
            pltpu.VMEM((4, 4, 2, 32, 256), BF),
            pltpu.VMEM((256, 1024), BF),
            pltpu.VMEM((4, 8, 128), F32),
            pltpu.VMEM((8, 32, 128), BF),
            pltpu.VMEM((4, 4, 2, 32, 128), BF),
            pltpu.VMEM((1024, 128), F32),
            pltpu.VMEM((16, 128, 256), BF),
            pltpu.VMEM((32, 32, 512), BF),
            pltpu.VMEM((2, 8, 16, 128), BF),
            pltpu.VMEM((2, 8, 16, 128), BF),
            pltpu.VMEM((2, 4, 128, 256), BF),
            pltpu.VMEM((2, 8, 4, 16, 256), BF),
            pltpu.VMEM((64, 256), F32),
            pltpu.VMEM((4, 16, 256), BF),
            pltpu.VMEM((32, 16, 256), BF),
            pltpu.VMEM((2, 512, 128), F32),
            pltpu.VMEM((1, 128), jnp.int32),
            pltpu.VMEM((32, 128), F32),
            pltpu.VMEM((4, 4, 16), jnp.int32),
            pltpu.VMEM((4, 4, 16), BF),
            pltpu.SemaphoreType.REGULAR((3,)),
            dma((12,)),
            dma((16,)), dma((16,)),
            dma((6,)), dma((2,)),
            dma((2, 7)), dma((2, 7)),
            dma((7,)), dma((7,)),
            dma((2, 7)), dma((2, 7)),
            dma((7,)), dma((7,)),
            dma((3, 19)), dma((3, 19)),
            dma((4,)), dma((32,)),
        ],
        compiler_params=pltpu.CompilerParams(
            collective_id=0, has_side_effects=True, vmem_limit_bytes=48 * 1024 * 1024
        ),
        name="bse_chebyshev",
    )(
        *[
            pltpu.with_memory_space_constraint(value, pltpu.HBM)
            for value in (
                screened, density, transform, trial, bands.reshape(1, 128), energy.reshape(32, 128),
                jnp.transpose(coarse_index, (0, 2, 1)), jnp.transpose(interp_weight, (0, 2, 1)),
            )
        ]
    )
    return pl.pallas_call(
        layout,
        out_shape=(jax.ShapeDtypeStruct((1024, 128), BF), jax.ShapeDtypeStruct((4096, 128), F32)),
        in_specs=[vmem] * 2,
        out_specs=(hbm, hbm),
        scratch_shapes=[pltpu.VMEM((2, 2048, 128), F32), pltpu.VMEM((4096, 128), F32), dma((5,))],
        compiler_params=pltpu.CompilerParams(vmem_limit_bytes=48 * 1024 * 1024),
        name="layout",
    )(first, gathered)


def solution(mesh):
    in_specs = (
        P("pair", "pw", None),
        P("pair", "pw", None),
        P("pw", None, None),
        P("pw"),
        P("pw", None),
        P("pair", "pw", None),
        P("pair", "pw", None),
        P(),
    )
    out_specs = (P("pair", None), P("pw", None))
    return jax.shard_map(shards, mesh=mesh, in_specs=in_specs, out_specs=out_specs, check_vma=False)
```
